32 devices in a mesh: gx: 4 (over z), gy: 8 (over y, x, core).
Axes of the slice: x: 2, y: 2, z: 4, core: 2. Of those that a mesh axis runs over, the one named last changes fastest.
Arguments:
- state_field: float32 [32, 32, 2048], P(None, 'gx', 'gy'), may hold values from -6 to 6
- spectral_weight: float32 [32, 32, 2, 32, 512], P('gx', 'gy'), may hold values from -6 to 6
- conv_fine: float32 [27, 32, 32], replicated, may hold values from -0.21875 to 0.21875
- conv_coarse: float32 [27, 32, 32], replicated, may hold values from -0.21875 to 0.21875
- conv_mix: float32 [32, 32], replicated, may hold values from -1 to 1
- linear_weight: float32 [32, 32], replicated, may hold values from -1 to 1
- bias_vector: float32 [32], replicated, may hold values from -3 to 3
Outputs:
- layer_out: float32 [32, 32, 2048], P(None, 'gx', 'gy')
The draws below stay inside these ranges and needn't reach their ends.
All inputs are finite; a program needn't handle non-finite values.
Results may differ from the reference program's by a relative error of at most 0.0001.
Values sent between devices are 32-bit elements; how exact they have to be, the bound alone decides.
A program may use at most 64 MiB of HBM per device.

```python
import jax
import jax.numpy as jnp
from jax import lax

C = 32
KX = 32
KY = 32
KZ = 16
NZ = 32
NX = 32
NY = 64


def block_scale(stream_key, shape, cuts, low, largest):
    def one(dim, shards_of):
        draws = jax.random.uniform(jax.random.fold_in(jax.random.fold_in(stream_key, 6), dim), (shards_of,), jnp.float32, low / len(cuts), largest / len(cuts))
        return jnp.repeat(jnp.exp(draws), shape[dim] // shards_of).reshape((-1,) + (1,) * (len(shape) - dim - 1))

    level = one(*cuts[0])
    for cut in cuts[1:]:
        level = level * one(*cut)
    return level


def bell_draw(key, extent, width, limit, shards=(), kind=jnp.bfloat16):
    factor_of = block_scale(key, extent, shards, -0.22, 0.18) if shards else 1.0
    values = jax.random.normal(key, extent, jnp.float32) * width * factor_of
    return jnp.minimum(jnp.maximum(values, -limit), limit).astype(kind)


def setup_inputs(seed: int = 0) -> dict:
    streams_of = jax.random.split(jax.random.key(seed), 8)
    return {
        "state_field": bell_draw(streams_of[0], (C, NX, NY * NZ), 1.0, 6.0, ((1, 4), (2, 8)), jnp.float32),
        "spectral_weight": bell_draw(streams_of[1], (KX, KY, 2, C, C * KZ), 1.0, 6.0, ((0, 4), (1, 8)), jnp.float32),
        "conv_fine": bell_draw(streams_of[2], (27, C, C), (27 * C) ** -0.5, 0.21875, (), jnp.float32),
        "conv_coarse": bell_draw(streams_of[3], (27, C, C), (27 * C) ** -0.5, 0.21875, (), jnp.float32),
        "conv_mix": bell_draw(streams_of[4], (C, C), C ** -0.5, 1.0, (), jnp.float32),
        "linear_weight": bell_draw(streams_of[5], (C, C), C ** -0.5, 1.0, (), jnp.float32),
        "bias_vector": bell_draw(streams_of[6], (C,), 0.5, 3.0, (), jnp.float32),
    }


exact_precision = lax.Precision.HIGHEST


def conv_three(volume, weight):
    channels, size_x, size_y, size_z = volume.shape
    padded = jnp.pad(volume, ((0, 0), (1, 1), (1, 1), (1, 1)))
    accumulated = jnp.zeros_like(volume)
    for offset in range(27):
        shift_x, shift_y, shift_z = offset // 9, (offset // 3) % 3, offset % 3
        window = padded[:, shift_x:shift_x + size_x, shift_y:shift_y + size_y, shift_z:shift_z + size_z]
        accumulated = accumulated + jnp.einsum('oi,ixyz->oxyz', weight[offset], window, precision=exact_precision)
    return accumulated


def pool_half(volume):
    channels, size_x, size_y, size_z = volume.shape
    blocks = volume.reshape(channels, size_x // 2, 2, size_y // 2, 2, size_z // 2, 2)
    return blocks.mean(axis=(2, 4, 6))


def upsample(volume):
    return jnp.repeat(jnp.repeat(jnp.repeat(volume, 2, axis=1), 2, axis=2), 2, axis=3)


def contract(values, kernel):
    return jnp.einsum('ixyz,xyioz->oxyz', values, kernel, precision=exact_precision)


def spectral(volume, spectral_weight):
    channels, size_x, size_y, size_z = volume.shape
    half_x, half_y = KX // 2, KY // 2
    spectrum = jnp.fft.rfftn(volume, axes=(1, 2, 3))
    retained = jnp.concatenate([spectrum[:, :half_x], spectrum[:, size_x - half_x:]], axis=1)
    retained = jnp.concatenate([retained[:, :, :half_y], retained[:, :, size_y - half_y:]], axis=2)
    retained = retained[:, :, :, :KZ]
    real_part = jnp.real(retained)
    imag_part = jnp.imag(retained)
    kernel = spectral_weight.reshape(KX, KY, 2, C, C, KZ)
    out_real = contract(real_part, kernel[:, :, 0]) - contract(imag_part, kernel[:, :, 1])
    out_imag = contract(real_part, kernel[:, :, 1]) + contract(imag_part, kernel[:, :, 0])
    modes = lax.complex(out_real, out_imag)
    zeros_x = jnp.zeros((channels, size_x - KX, KY, KZ), modes.dtype)
    modes = jnp.concatenate([modes[:, :half_x], zeros_x, modes[:, half_x:]], axis=1)
    zeros_y = jnp.zeros((channels, size_x, size_y - KY, KZ), modes.dtype)
    modes = jnp.concatenate([modes[:, :, :half_y], zeros_y, modes[:, :, half_y:]], axis=2)
    modes = jnp.pad(modes, ((0, 0), (0, 0), (0, 0), (0, size_z // 2 + 1 - KZ)))
    return jnp.fft.irfftn(modes, s=(size_x, size_y, size_z), axes=(1, 2, 3))


def reference(state_field, spectral_weight, conv_fine, conv_coarse, conv_mix, linear_weight, bias_vector):
    volume = state_field.reshape(C, NX, NY, NZ)
    fourier = spectral(volume, spectral_weight)
    fine_level = jax.nn.gelu(conv_three(volume, conv_fine))
    coarse = jax.nn.gelu(conv_three(pool_half(fine_level), conv_coarse))
    joined = fine_level + upsample(coarse)
    unet_branch = jnp.einsum('oi,ixyz->oxyz', conv_mix, joined, precision=exact_precision)
    pointwise = jnp.einsum('oi,ixyz->oxyz', linear_weight, volume, precision=exact_precision)
    summed = fourier + unet_branch + pointwise + bias_vector[:, None, None, None]
    return jax.nn.gelu(summed).reshape(C, NX, NY * NZ)
```

```python
import functools
import math

import jax
import jax.numpy as jnp
import numpy as np
from jax import lax
from jax.experimental import pallas as pl
from jax.experimental.pallas import tpu as pltpu
from jax.sharding import PartitionSpec as P

KX = 32
KY = 32
KZ = 16
NZ = 32


exact_precision = lax.Precision.HIGH


def extended(cells, sides, width):
    for axis, dim in sides:
        count = lax.axis_size(axis)
        ends = count - 1
        head = lax.slice_in_dim(cells, 0, width, axis=dim)
        tail = lax.slice_in_dim(cells, cells.shape[dim] - width, cells.shape[dim], axis=dim)
        cells = jnp.concatenate(
            [
                lax.ppermute(tail, axis, [(i, (i + 1) % count) for i in range(ends)]),
                cells,
                lax.ppermute(head, axis, [((i + 1) % count, i) for i in range(ends)]),
            ],
            axis=dim,
        )
    return cells


def mode_frequency(count, length):
    indices = jnp.arange(count, dtype=jnp.int32)
    return jnp.where(indices < count // 2, indices, indices - count + length)


def forward_table(count, length, start, cells):
    frequency = mode_frequency(count, length)
    places = start + jnp.arange(cells, dtype=jnp.int32)
    phase = frequency[:, None] * places[None, :] % length
    angles = phase.astype(jnp.float32) * (2.0 * math.pi / length)
    cosines = jnp.cos(angles)
    sines = jnp.sin(angles)
    upper_rows = jnp.stack([cosines, sines], axis=-1)
    lower_rows = jnp.stack([-sines, cosines], axis=-1)
    return jnp.stack([upper_rows, lower_rows], axis=1)


def conv_merged(padded, weight, cells_x, cells_y, depth):
    channels = padded.shape[0]
    flat = padded.reshape(channels, cells_x + 2, (cells_y + 2) * depth)
    flat = jnp.pad(flat, ((0, 0), (0, 0), (1, 1)))
    width = cells_y * depth
    positions = jnp.arange(width, dtype=jnp.int32) % depth
    lower_keep = (positions > 0).astype(jnp.float32)
    upper_keep = (positions < depth - 1).astype(jnp.float32)
    accumulated = jnp.zeros((channels, cells_x, width), jnp.float32)
    for offset in range(27):
        shift_x, shift_y, shift_z = (offset // 9, offset // 3 % 3, offset % 3)
        start = shift_y * depth + shift_z
        window = flat[:, shift_x : shift_x + cells_x, start : start + width]
        term = jnp.einsum("oi,ixw->oxw", weight[offset], window, precision=exact_precision)
        if shift_z == 0:
            term = term * lower_keep
        elif shift_z == 2:
            term = term * upper_keep
        accumulated = accumulated + term
    return accumulated


def contract(values, kernel):
    return jnp.einsum("xyiz,xyioz->xyoz", values, kernel, precision=exact_precision)


def mix_modes(owned_modes, spectral_weight, channels):
    rows_x, rows_y = (owned_modes.shape[0], owned_modes.shape[1])
    values = owned_modes.reshape(rows_x, rows_y, 2, channels, KZ)
    kernel = spectral_weight.reshape(rows_x, rows_y, 2, channels, channels, KZ)
    real_part = contract(values[:, :, 0], kernel[:, :, 0]) - contract(
        values[:, :, 1], kernel[:, :, 1]
    )
    imag_part = contract(values[:, :, 0], kernel[:, :, 1]) + contract(
        values[:, :, 1], kernel[:, :, 0]
    )
    return jnp.stack([real_part, imag_part], axis=2).reshape(rows_x, rows_y, 2, channels * KZ)


MESH = pl.DeviceIdType.MESH


def split_pair(values):
    high = values.astype(jnp.bfloat16)
    return high, (values - high.astype(jnp.float32)).astype(jnp.bfloat16)


def dot_split(left, high, low):
    left_high, left_low = split_pair(left)
    dot = functools.partial(jnp.dot, preferred_element_type=jnp.float32)
    return dot(left_high, high) + dot(left_high, low) + dot(left_low, high)


def host_pair(values):
    high = values.astype(np.float32).astype(jnp.bfloat16)
    low = (values - high.astype(np.float64)).astype(np.float32).astype(jnp.bfloat16)
    return jnp.asarray(high), jnp.asarray(low)


def host_frequency(count, length):
    indices = np.arange(count)
    return np.where(indices < count // 2, indices, indices - count + length)


def spectral_tables(groups_x, groups_y, cells_x, cells_y, rows_y):
    total_x, total_y = groups_x * cells_x, groups_y * cells_y
    fy = host_frequency(KY, total_y)
    places = np.arange(cells_y)
    kz = np.arange(KZ)
    zs = np.arange(NZ)
    turn_y = places[:, None] * fy[None, :] % total_y / total_y
    turn_z = zs[:, None] * kz[None, :] % NZ / NZ
    angle = 2 * np.pi * (turn_y[:, None, :, None] + turn_z[None, :, None, :])
    table = np.stack([np.cos(angle), -np.sin(angle)], axis=2)
    table = table.reshape(cells_y * NZ, 2, groups_y, rows_y, KZ).transpose(2, 0, 1, 3, 4)
    table = table.reshape(groups_y, cells_y * NZ, 2 * rows_y * KZ)
    scale = np.tile(np.where(kz == 0, 1.0, 2.0) / (total_x * total_y * NZ), 2 * rows_y)
    inverse = (table * scale).transpose(0, 2, 1)
    starts = np.arange(groups_y) * cells_y
    phase = 2 * np.pi * (starts[:, None] * fy[None, :] % total_y) / total_y
    phase = np.broadcast_to(phase.reshape(-1, 1, rows_y, 1), (groups_y**2, 2, rows_y, KZ))
    signs = np.array([1.0, -1.0]).reshape(1, 2, 1, 1)
    rotation = np.stack([np.cos(phase), signs * np.sin(phase)], axis=1)
    rotation = rotation.reshape(groups_y**2, 2, 2 * rows_y * KZ).astype(np.float32)
    fx = host_frequency(KX, total_x)
    angle_x = 2 * np.pi * (fx[:, None] * np.arange(total_x)[None, :] % total_x) / total_x
    table_x = np.stack([np.cos(angle_x), np.sin(angle_x)]).reshape(-1).astype(np.float32)
    return (*host_pair(table), *host_pair(inverse), jnp.asarray(rotation), jnp.asarray(table_x))


def lane_group(shape, axis, width):
    return lax.broadcasted_iota(jnp.int32, shape, axis) // width


def spectral_kernel(
    groups_x, groups_y, cells_x, rows_x, rows_y, channels,
    cells_ref, fwd_high, fwd_low, inv_high, inv_low, rotation, table_x, weight_hbm,
    out_ref,
    parts, parts_in, line, line_in, mixed, mixed_in, back, back_in, weight,
    send_sem, recv_sem, weight_sem,
):
    mx, my = lax.axis_index("gx"), lax.axis_index("gy")
    lanes = 2 * rows_y * KZ
    groups = 2 * rows_y
    total_x = groups_x * cells_x
    load_weight = pltpu.make_async_copy(weight_hbm, weight, weight_sem)
    load_weight.start()
    barrier = pltpu.get_barrier_semaphore()
    for step in range(1, groups_y):
        pl.semaphore_signal(
            barrier, inc=1, device_id=(mx, lax.rem(my + step, groups_y)), device_id_type=MESH
        )
    for step in range(1, groups_x):
        pl.semaphore_signal(
            barrier, inc=1, device_id=(lax.rem(mx + step, groups_x), my), device_id_type=MESH
        )
    pl.semaphore_wait(barrier, groups_x + groups_y - 2)

    def send(phase, step, source, target, device):
        copy = pltpu.make_async_remote_copy(
            src_ref=source, dst_ref=target,
            send_sem=send_sem.at[phase, step], recv_sem=recv_sem.at[phase, step],
            device_id=device, device_id_type=MESH,
        )
        copy.start()
        return copy

    half = lanes // 2
    left_high, left_low = split_pair(cells_ref[...])
    dot = functools.partial(jnp.dot, preferred_element_type=jnp.float32)
    copies = []
    for step in list(range(1, groups_y)) + [0]:
        peer = lax.rem(my + step, groups_y)
        high, low = fwd_high[peer], fwd_low[peer]
        part = dot(left_high, high) + dot(left_high, low) + dot(left_low, high)
        turn = rotation[my * groups_y + peer]
        part = part * turn[0:1] + pltpu.roll(part, half, 1) * turn[1:2]
        parts[step] = part
        if step:
            copies.append(send(0, step, parts.at[step], parts_in.at[step], (mx, peer)))
    total = parts[0]
    for step, copy in enumerate(copies, 1):
        copy.wait()
        total = total + parts_in[step]
    line[...] = total
    copies = [
        send(1, step, line, line_in.at[step], (lax.rem(mx + step, groups_x), my))
        for step in range(1, groups_x)
    ]
    for copy in copies:
        copy.wait()
    load_weight.wait()
    lane = lax.broadcasted_iota(jnp.int32, (channels, lanes), 1)
    sign = jnp.where(lane < half, 1.0, -1.0).astype(jnp.float32)
    group = lane // KZ
    row_8 = lax.broadcasted_iota(jnp.int32, (groups, lanes), 0)
    diagonal = lax.rem(row_8 - lax.broadcasted_iota(jnp.int32, (groups, lanes), 1) // KZ + groups, groups)

    def spread(values, index):
        picked = jnp.where(group == index, values, 0.0)
        shift = KZ
        while shift < lanes:
            picked = picked + pltpu.roll(picked, shift, 1)
            shift *= 2
        return picked

    def along_x(own, others, rows, place):
        first = jnp.zeros((channels, lanes), jnp.float32)
        second = jnp.zeros((channels, lanes), jnp.float32)
        for step in range(groups_x):
            base = lax.rem(mx - step + groups_x, groups_x) * rows
            for row in range(rows):
                position = place(base + row)
                block = pl.ds(row * channels, channels)
                values = own[block, :] if step == 0 else others[step, block, :]
                first = first + values * table_x[position]
                second = second + values * table_x[KX * total_x + position]
        return first, pltpu.roll(second, half, 1) * sign

    def one_mode(j, carry):
        first, second = along_x(line, line_in, cells_x, lambda x: (mx * rows_x + j) * total_x + x)
        modes = first + second
        tiles = channels * KZ // lanes
        rows = [jnp.zeros((groups, lanes), jnp.float32) for _ in range(tiles)]
        for k in range(rows_y):
            real, imag = spread(modes, k), spread(modes, rows_y + k)
            for tile in range(tiles):
                columns = pl.ds(tile * lanes, lanes)
                w_real = weight[j, k, 0, :, columns]
                w_imag = weight[j, k, 1, :, columns]
                out_real = jnp.sum(real * w_real - imag * w_imag, axis=0, keepdims=True)
                out_imag = jnp.sum(real * w_imag + imag * w_real, axis=0, keepdims=True)
                rows[tile] = jnp.where(row_8 == k, out_real, rows[tile])
                rows[tile] = jnp.where(row_8 == rows_y + k, out_imag, rows[tile])
        for tile in range(tiles):
            turned = jnp.where(diagonal == 0, rows[tile], 0.0)
            for d in range(1, groups):
                moved = pltpu.roll(pltpu.roll(rows[tile], d, 0), lanes - KZ * d, 1)
                turned = jnp.where(diagonal == d, moved, turned)
            start = pl.multiple_of(j * channels + tile * groups, groups)
            mixed[pl.ds(start, groups), :] = turned
        return carry

    lax.fori_loop(0, rows_x, one_mode, 0)
    copies = [
        send(2, step, mixed, mixed_in.at[step], (lax.rem(mx + step, groups_x), my))
        for step in range(1, groups_x)
    ]
    for copy in copies:
        copy.wait()

    def one_line(j, carry):
        first, second = along_x(mixed, mixed_in, rows_x, lambda k: k * total_x + mx * cells_x + j)
        back[pl.ds(pl.multiple_of(j * channels, channels), channels), :] = first - second
        return carry

    lax.fori_loop(0, cells_x, one_line, 0)
    copies = [
        send(3, step, back, back_in.at[step], (mx, lax.rem(my + step, groups_y)))
        for step in range(1, groups_y)
    ]
    result = None
    for step in range(groups_y):
        if step:
            copies[step - 1].wait()
        values = back_in[step] if step else back[...]
        peer = lax.rem(my - step + groups_y, groups_y)
        turn = rotation[my * groups_y + peer]
        values = values * turn[0:1] - pltpu.roll(values, half, 1) * turn[1:2]
        term = dot_split(values, inv_high[peer], inv_low[peer])
        result = term if result is None else result + term
    out_ref[...] = result


def spectral(cells, spectral_weight, cells_y):
    cells_x, channels, plane = cells.shape
    rows_x, rows_y = spectral_weight.shape[:2]
    groups_x, groups_y = lax.axis_size("gx"), lax.axis_size("gy")
    lanes = 2 * rows_y * KZ
    tables = spectral_tables(groups_x, groups_y, cells_x, cells_y, rows_y)
    slab_x, slab_k = (cells_x * channels, lanes), (rows_x * channels, lanes)
    f32 = jnp.float32
    vmem = pl.BlockSpec(memory_space=pltpu.VMEM)
    return pl.pallas_call(
        functools.partial(
            spectral_kernel, groups_x, groups_y, cells_x, rows_x, rows_y, channels
        ),
        out_shape=jax.ShapeDtypeStruct((cells_x * channels, plane), f32),
        in_specs=[vmem] * 6
        + [pl.BlockSpec(memory_space=pltpu.SMEM), pl.BlockSpec(memory_space=pl.ANY)],
        out_specs=vmem,
        scratch_shapes=[
            pltpu.VMEM((groups_y, *slab_x), f32),
            pltpu.VMEM((groups_y, *slab_x), f32),
            pltpu.VMEM(slab_x, f32),
            pltpu.VMEM((groups_x, *slab_x), f32),
            pltpu.VMEM(slab_k, f32),
            pltpu.VMEM((groups_x, *slab_k), f32),
            pltpu.VMEM(slab_x, f32),
            pltpu.VMEM((groups_y, *slab_x), f32),
            pltpu.VMEM(spectral_weight.shape, f32),
            pltpu.SemaphoreType.DMA((4, max(groups_x, groups_y))),
            pltpu.SemaphoreType.DMA((4, max(groups_x, groups_y))),
            pltpu.SemaphoreType.DMA,
        ],
        compiler_params=pltpu.CompilerParams(
            collective_id=0, has_side_effects=True, vmem_limit_bytes=32 * 1024 * 1024
        ),
    )(cells.reshape(cells_x * channels, plane), *tables, spectral_weight)


def spectral_general(volume, spectral_weight):
    channels, cells_x, cells_y, _ = volume.shape
    total_x = cells_x * lax.axis_size("gx")
    total_y = cells_y * lax.axis_size("gy")
    merged = channels * KZ
    depth_modes = jnp.arange(KZ, dtype=jnp.int32)
    depth_cells = jnp.arange(NZ, dtype=jnp.int32)
    depth_angles = (depth_cells[:, None] * depth_modes[None, :] % NZ).astype(jnp.float32) * (
        2.0 * math.pi / NZ
    )
    depth_forward = jnp.stack([jnp.cos(depth_angles), -jnp.sin(depth_angles)], axis=1)
    along_z = jnp.einsum("cxyz,zqk->xyqck", volume, depth_forward, precision=exact_precision)
    along_z = along_z.reshape(cells_x, cells_y, 2, merged)
    table_x = forward_table(KX, total_x, lax.axis_index("gx") * cells_x, cells_x)
    table_y = forward_table(KY, total_y, lax.axis_index("gy") * cells_y, cells_y)
    inverse_x = jnp.transpose(table_x, (2, 3, 0, 1))
    inverse_y = jnp.transpose(table_y, (2, 3, 0, 1))
    part_x = jnp.einsum("kpxq,xyqm->kypm", table_x, along_z, precision=exact_precision)
    summed_x = lax.psum_scatter(part_x, "gx", scatter_dimension=0, tiled=True)
    partials = jnp.einsum("jpyq,kyqm->kjpm", table_y, summed_x, precision=exact_precision)
    owned_modes = lax.psum_scatter(partials, "gy", scatter_dimension=1, tiled=True)
    mixed_modes = mix_modes(owned_modes, spectral_weight, channels)
    whole_y = lax.all_gather(mixed_modes, "gy", axis=1, tiled=True)
    back_y = jnp.einsum("ypjq,kjqm->kypm", inverse_y, whole_y, precision=exact_precision)
    whole_x = lax.all_gather(back_y, "gx", axis=0, tiled=True)
    back_x = jnp.einsum("xpkq,kyqm->xypm", inverse_x, whole_x, precision=exact_precision)
    weights_z = jnp.where(depth_modes == 0, 1.0, 2.0).astype(jnp.float32) / (total_x * total_y * NZ)
    inverse_angles = jnp.transpose(depth_angles)
    depth_inverse = jnp.stack(
        [
            weights_z[:, None] * jnp.cos(inverse_angles),
            -weights_z[:, None] * jnp.sin(inverse_angles),
        ],
        axis=0,
    )
    fourier = jnp.einsum(
        "xyqck,qkz->cxyz",
        back_x.reshape(cells_x, cells_y, 2, channels, KZ),
        depth_inverse,
        precision=exact_precision,
    )
    return fourier.reshape(channels, cells_x, cells_y * NZ)


def per_device(
    state_field, spectral_weight, conv_fine, conv_coarse, conv_mix, linear_weight, bias_vector
):
    channels, cells_x, plane = state_field.shape
    cells_y = plane // NZ
    volume = state_field.reshape(channels, cells_x, cells_y, NZ)
    padded = extended(volume, (("gx", 1), ("gy", 2)), 1)
    fine_level = jax.nn.gelu(conv_merged(padded, conv_fine, cells_x, cells_y, NZ))
    pooled = fine_level.reshape(channels, cells_x // 2, 2, cells_y // 2, 2, NZ // 2, 2).mean(
        axis=(2, 4, 6)
    )
    coarse_padded = extended(pooled, (("gx", 1), ("gy", 2)), 1)
    coarse = jax.nn.gelu(
        conv_merged(coarse_padded, conv_coarse, cells_x // 2, cells_y // 2, NZ // 2)
    )
    coarse = coarse.reshape(channels, cells_x // 2, 1, cells_y // 2, 1, NZ // 2, 1)
    spread = jnp.broadcast_to(coarse, (channels, cells_x // 2, 2, cells_y // 2, 2, NZ // 2, 2))
    joined = fine_level + spread.reshape(channels, cells_x, cells_y * NZ)
    unet_branch = jnp.einsum("oi,ixw->oxw", conv_mix, joined, precision=exact_precision)
    pointwise = jnp.einsum("oi,ixw->oxw", linear_weight, state_field, precision=exact_precision)
    rows_y = spectral_weight.shape[1]
    if 2 * rows_y * KZ == 128 and 2 * rows_y == 8 and channels % 8 == 0 and plane % 128 == 0:
        cells = jnp.transpose(state_field, (1, 0, 2))
        fourier = spectral(cells, spectral_weight, cells_y)
        fourier = jnp.transpose(fourier.reshape(cells_x, channels, plane), (1, 0, 2))
    else:
        fourier = spectral_general(volume, spectral_weight)
    summed = fourier + unet_branch + pointwise + bias_vector[:, None, None]
    return jax.nn.gelu(summed)


def solution(mesh):
    placed = (P(None, "gx", "gy"), P("gx", "gy", None, None, None), P(), P(), P(), P(), P())
    return jax.shard_map(
        per_device, mesh=mesh, in_specs=placed, out_specs=P(None, "gx", "gy"), check_vma=False
    )
```

```python
import functools
import math

import jax
import jax.numpy as jnp
import numpy as np
from jax import lax
from jax.experimental import pallas as pl
from jax.experimental.pallas import tpu as pltpu
from jax.sharding import PartitionSpec as P

KX = 32
KY = 32
KZ = 16
NZ = 32


exact_precision = lax.Precision.HIGH


def extended(cells, sides, width):
    for axis, dim in sides:
        count = lax.axis_size(axis)
        ends = count - 1
        head = lax.slice_in_dim(cells, 0, width, axis=dim)
        tail = lax.slice_in_dim(cells, cells.shape[dim] - width, cells.shape[dim], axis=dim)
        cells = jnp.concatenate(
            [
                lax.ppermute(tail, axis, [(i, (i + 1) % count) for i in range(ends)]),
                cells,
                lax.ppermute(head, axis, [((i + 1) % count, i) for i in range(ends)]),
            ],
            axis=dim,
        )
    return cells


def mode_frequency(count, length):
    indices = jnp.arange(count, dtype=jnp.int32)
    return jnp.where(indices < count // 2, indices, indices - count + length)


def forward_table(count, length, start, cells):
    frequency = mode_frequency(count, length)
    places = start + jnp.arange(cells, dtype=jnp.int32)
    phase = frequency[:, None] * places[None, :] % length
    angles = phase.astype(jnp.float32) * (2.0 * math.pi / length)
    cosines = jnp.cos(angles)
    sines = jnp.sin(angles)
    upper_rows = jnp.stack([cosines, sines], axis=-1)
    lower_rows = jnp.stack([-sines, cosines], axis=-1)
    return jnp.stack([upper_rows, lower_rows], axis=1)


def conv_merged(padded, weight, cells_x, cells_y, depth):
    channels = padded.shape[0]
    flat = padded.reshape(channels, cells_x + 2, (cells_y + 2) * depth)
    flat = jnp.pad(flat, ((0, 0), (0, 0), (1, 1)))
    width = cells_y * depth
    positions = jnp.arange(width, dtype=jnp.int32) % depth
    lower_keep = (positions > 0).astype(jnp.float32)
    upper_keep = (positions < depth - 1).astype(jnp.float32)
    accumulated = jnp.zeros((channels, cells_x, width), jnp.float32)
    for offset in range(27):
        shift_x, shift_y, shift_z = (offset // 9, offset // 3 % 3, offset % 3)
        start = shift_y * depth + shift_z
        window = flat[:, shift_x : shift_x + cells_x, start : start + width]
        term = jnp.einsum("oi,ixw->oxw", weight[offset], window, precision=exact_precision)
        if shift_z == 0:
            term = term * lower_keep
        elif shift_z == 2:
            term = term * upper_keep
        accumulated = accumulated + term
    return accumulated


def contract(values, kernel):
    return jnp.einsum("xyiz,xyioz->xyoz", values, kernel, precision=exact_precision)


def mix_modes(owned_modes, spectral_weight, channels):
    rows_x, rows_y = (owned_modes.shape[0], owned_modes.shape[1])
    values = owned_modes.reshape(rows_x, rows_y, 2, channels, KZ)
    kernel = spectral_weight.reshape(rows_x, rows_y, 2, channels, channels, KZ)
    real_part = contract(values[:, :, 0], kernel[:, :, 0]) - contract(
        values[:, :, 1], kernel[:, :, 1]
    )
    imag_part = contract(values[:, :, 0], kernel[:, :, 1]) + contract(
        values[:, :, 1], kernel[:, :, 0]
    )
    return jnp.stack([real_part, imag_part], axis=2).reshape(rows_x, rows_y, 2, channels * KZ)


MESH = pl.DeviceIdType.MESH


def split_pair(values):
    high = values.astype(jnp.bfloat16)
    return high, (values - high.astype(jnp.float32)).astype(jnp.bfloat16)


def dot_split(left, high, low):
    left_high, left_low = split_pair(left)
    dot = functools.partial(jnp.dot, preferred_element_type=jnp.float32)
    return dot(left_high, high) + dot(left_high, low) + dot(left_low, high)


def host_pair(values):
    high = values.astype(np.float32).astype(jnp.bfloat16)
    low = (values - high.astype(np.float64)).astype(np.float32).astype(jnp.bfloat16)
    return jnp.asarray(high), jnp.asarray(low)


def host_frequency(count, length):
    indices = np.arange(count)
    return np.where(indices < count // 2, indices, indices - count + length)


def spectral_tables(groups_x, groups_y, cells_x, cells_y, rows_y):
    total_x, total_y = groups_x * cells_x, groups_y * cells_y
    fy = host_frequency(KY, total_y)
    places = np.arange(cells_y)
    kz = np.arange(KZ)
    zs = np.arange(NZ)
    turn_y = places[:, None] * fy[None, :] % total_y / total_y
    turn_z = zs[:, None] * kz[None, :] % NZ / NZ
    angle = 2 * np.pi * (turn_y[:, None, :, None] + turn_z[None, :, None, :])
    table = np.stack([np.cos(angle), -np.sin(angle)], axis=2)
    table = table.reshape(cells_y * NZ, 2, groups_y, rows_y, KZ).transpose(2, 0, 1, 3, 4)
    table = table.reshape(groups_y, cells_y * NZ, 2 * rows_y * KZ)
    scale = np.tile(np.where(kz == 0, 1.0, 2.0) / (total_x * total_y * NZ), 2 * rows_y)
    inverse = (table * scale).transpose(0, 2, 1)
    starts = np.arange(groups_y) * cells_y
    phase = 2 * np.pi * (starts[:, None] * fy[None, :] % total_y) / total_y
    phase = np.broadcast_to(phase.reshape(-1, 1, rows_y, 1), (groups_y**2, 2, rows_y, KZ))
    signs = np.array([1.0, -1.0]).reshape(1, 2, 1, 1)
    rotation = np.stack([np.cos(phase), signs * np.sin(phase)], axis=1)
    rotation = rotation.reshape(groups_y**2, 2, 2 * rows_y * KZ).astype(np.float32)
    fx = host_frequency(KX, total_x)
    angle_x = 2 * np.pi * (fx[:, None] * np.arange(total_x)[None, :] % total_x) / total_x
    table_x = np.stack([np.cos(angle_x), np.sin(angle_x)]).reshape(-1).astype(np.float32)
    return (*host_pair(table), *host_pair(inverse), jnp.asarray(rotation), jnp.asarray(table_x))


def lane_group(shape, axis, width):
    return lax.broadcasted_iota(jnp.int32, shape, axis) // width


def spectral_kernel(
    groups_x, groups_y, cells_x, rows_x, rows_y, channels,
    cells_ref, fwd_high, fwd_low, inv_high, inv_low, rotation, table_x, weight_hbm,
    fine_ref, coarse_ref, point_ref, bias_ref, pool_ref, spread_ref,
    out_ref,
    parts, parts_in, line, line_in, mixed, mixed_in, back, back_in, weight,
    send_sem, recv_sem, weight_sem,
    edges, edges_in, planes_in, corners_in, padded, stack_high, stack_low, sums, fine,
    pooled, rim, rim_in, pooled_in, rim_corners_in, coarse_padded, base,
    halo_send, halo_recv,
):
    mx, my = lax.axis_index("gx"), lax.axis_index("gy")
    lanes = 2 * rows_y * KZ
    groups = 2 * rows_y
    total_x = groups_x * cells_x
    load_weight = pltpu.make_async_copy(weight_hbm, weight, weight_sem)
    load_weight.start()
    barrier = pltpu.get_barrier_semaphore()
    for step in range(1, groups_y):
        pl.semaphore_signal(
            barrier, inc=1, device_id=(mx, lax.rem(my + step, groups_y)), device_id_type=MESH
        )
    for step in range(1, groups_x):
        pl.semaphore_signal(
            barrier, inc=1, device_id=(lax.rem(mx + step, groups_x), my), device_id_type=MESH
        )
    up_x, down_x = lax.rem(mx + 1, groups_x), lax.rem(mx + groups_x - 1, groups_x)
    up_y, down_y = lax.rem(my + 1, groups_y), lax.rem(my + groups_y - 1, groups_y)
    sides_x, sides_y = (down_x, up_x), (down_y, up_y)
    for to_x in sides_x:
        for to_y in sides_y:
            pl.semaphore_signal(barrier, inc=1, device_id=(to_x, to_y), device_id_type=MESH)
    pl.semaphore_wait(barrier, groups_x + groups_y + 2)

    def halo(phase, index, source, target, device):
        copy = pltpu.make_async_remote_copy(
            src_ref=source, dst_ref=target,
            send_sem=halo_send.at[phase, index], recv_sem=halo_recv.at[phase, index],
            device_id=device, device_id_type=MESH,
        )
        copy.start()
        return copy

    def rows_of(plane):
        return pl.ds(plane * channels, channels)

    lane_full = lax.broadcasted_iota(jnp.int32, (channels, 128), 1)
    plane_lanes = cells_ref.shape[1]
    per_tile = 128 // NZ
    last_tile = cells_x // per_tile - 1
    for tile in range(cells_x // per_tile):
        first = jnp.zeros((channels, 128), jnp.float32)
        last = jnp.zeros((channels, 128), jnp.float32)
        for slot in range(per_tile):
            rows = rows_of(tile * per_tile + slot)
            here = lane_full // NZ == slot
            head = cells_ref[rows, 0:128]
            tail = cells_ref[rows, plane_lanes - 128 : plane_lanes]
            first = jnp.where(here, pltpu.roll(head, slot * NZ, 1), first)
            last = jnp.where(here, pltpu.roll(tail, (slot * NZ + NZ) % 128, 1), last)
        edges[0, tile] = first
        edges[1, tile] = last
    halos = []
    for side in range(2):
        edge_plane = cells_ref.at[rows_of(side * (cells_x - 1)), :]
        halos.append(halo(0, side, edge_plane, planes_in.at[1 - side], (sides_x[side], my)))
        halos.append(halo(0, 2 + side, edges.at[side], edges_in.at[1 - side], (mx, sides_y[side])))
        for other in range(2):
            halos.append(
                halo(
                    0, 4 + 2 * side + other, edges.at[other, side * last_tile],
                    corners_in.at[1 - side, 1 - other], (sides_x[side], sides_y[other]),
                )
            )

    def send(phase, step, source, target, device):
        copy = pltpu.make_async_remote_copy(
            src_ref=source, dst_ref=target,
            send_sem=send_sem.at[phase, step], recv_sem=recv_sem.at[phase, step],
            device_id=device, device_id_type=MESH,
        )
        copy.start()
        return copy

    half = lanes // 2
    left_high, left_low = split_pair(cells_ref[...])
    dot = functools.partial(jnp.dot, preferred_element_type=jnp.float32)
    copies = []
    for step in list(range(1, groups_y)) + [0]:
        peer = lax.rem(my + step, groups_y)
        high, low = fwd_high[peer], fwd_low[peer]
        part = dot(left_high, high) + dot(left_high, low) + dot(left_low, high)
        turn = rotation[my * groups_y + peer]
        part = part * turn[0:1] + pltpu.roll(part, half, 1) * turn[1:2]
        parts[step] = part
        if step:
            copies.append(send(0, step, parts.at[step], parts_in.at[step], (mx, peer)))
    f32 = jnp.float32
    at_x = ((mx > 0).astype(f32), (mx < groups_x - 1).astype(f32))
    at_y = ((my > 0).astype(f32), (my < groups_y - 1).astype(f32))
    for copy in halos:
        copy.wait()

    def fill(plane, main, left, right, left_slot, right_slot, scale):
        padded[plane, :, 0:128] = (
            pltpu.roll(left, (128 - NZ - left_slot * NZ) % 128, 1) * (at_y[0] * scale)
        )
        padded[plane, :, 128 : 128 + plane_lanes] = main * scale
        padded[plane, :, 128 + plane_lanes : 256 + plane_lanes] = (
            pltpu.roll(right, (128 - right_slot * NZ) % 128, 1) * (at_y[1] * scale)
        )

    for x in range(cells_x):
        tile, slot = x // per_tile, x % per_tile
        fill(x + 1, cells_ref[rows_of(x), :], edges_in[0, tile], edges_in[1, tile], slot, slot, 1.0)
    end = per_tile - 1
    fill(0, planes_in[0], corners_in[0, 0], corners_in[0, 1], end, end, at_x[0])
    fill(cells_x + 1, planes_in[1], corners_in[1, 0], corners_in[1, 1], 0, 0, at_x[1])

    def convolve(source, kernel, count, width, start, depth):
        kernel_high, kernel_low = split_pair(kernel)
        total_lanes = source.shape[2]
        depths = lax.broadcasted_iota(jnp.int32, (channels, width), 1) % depth
        for slot in range(count + 4):
            sums[slot, :, 0:width] = jnp.zeros((channels, width), f32)

        def one_plane(plane, carry):
            values = source[plane]
            for tap in range(9):
                shift_y, shift_z = tap // 3 - 1, tap % 3 - 1
                moved = pltpu.roll(values, (-shift_y * depth - shift_z) % total_lanes, 1)
                moved = moved[:, start : start + width]
                if shift_z == -1:
                    moved = jnp.where(depths > 0, moved, 0.0)
                elif shift_z == 1:
                    moved = jnp.where(depths < depth - 1, moved, 0.0)
                high, low = split_pair(moved)
                stack_high[tap * channels : (tap + 1) * channels, 0:width] = high
                stack_low[tap * channels : (tap + 1) * channels, 0:width] = low
            high, low = stack_high[:, 0:width], stack_low[:, 0:width]
            term = dot(kernel_high, high) + dot(kernel_high, low) + dot(kernel_low, high)
            for shift_x in range(3):
                piece = term[shift_x * channels : (shift_x + 1) * channels]
                slot = plane - shift_x + 2
                sums[slot, :, 0:width] = sums[slot, :, 0:width] + piece
            return carry

        lax.fori_loop(0, count + 2, one_plane, 0)

    convolve(padded, fine_ref[...], cells_x, plane_lanes, 128, NZ)
    pairs = cells_x // 2
    short = NZ // 2
    for x in range(cells_x):
        fine[x] = jax.nn.gelu(sums[x + 2])
    for pair in range(pairs):
        high, low = split_pair(fine[2 * pair] + fine[2 * pair + 1])
        pooled[pair] = dot(high, pool_ref[...]) + dot(low, pool_ref[...])
    packed = jnp.zeros((channels, 128), f32)
    for pair in range(pairs):
        values = pooled[pair]
        slot = lane_full // short
        packed = jnp.where(slot == pair, pltpu.roll(values, (pair * short - short) % 128, 1), packed)
        packed = jnp.where(slot == pairs + pair, pltpu.roll(values, pair * short, 1), packed)
    rim[...] = packed
    rims = []
    for side in range(2):
        rims.append(
            halo(1, side, pooled.at[side * (pairs - 1)], pooled_in.at[1 - side], (sides_x[side], my))
        )
        rims.append(halo(1, 2 + side, rim, rim_in.at[1 - side], (mx, sides_y[side])))
        for other in range(2):
            rims.append(
                halo(
                    1, 4 + 2 * side + other, rim, rim_corners_in.at[1 - side, 1 - other],
                    (sides_x[side], sides_y[other]),
                )
            )
    total = parts[0]
    for step, copy in enumerate(copies, 1):
        copy.wait()
        total = total + parts_in[step]
    line[...] = total
    copies = [
        send(1, step, line, line_in.at[step], (lax.rem(mx + step, groups_x), my))
        for step in range(1, groups_x)
    ]
    for copy in rims:
        copy.wait()
    inner = short * (pairs + 1)

    def fill_coarse(plane, main, left, right, slot, scale):
        before = pltpu.roll(left, (128 - (pairs + slot) * short) % 128, 1) * at_y[0]
        after = pltpu.roll(right, (inner - slot * short) % 128, 1) * at_y[1]
        values = jnp.where(lane_full < short, before, main)
        values = jnp.where(lane_full // short == pairs + 1, after, values)
        coarse_padded[plane] = values * scale

    for pair in range(pairs):
        fill_coarse(pair + 1, pooled[pair], rim_in[0], rim_in[1], pair, 1.0)
    fill_coarse(0, pooled_in[0], rim_corners_in[0, 0], rim_corners_in[0, 1], pairs - 1, at_x[0])
    fill_coarse(pairs + 1, pooled_in[1], rim_corners_in[1, 0], rim_corners_in[1, 1], 0, at_x[1])
    convolve(coarse_padded, coarse_ref[...], pairs, 128, 0, short)
    point_high, point_low = split_pair(point_ref[...])
    for pair in range(pairs):
        high, low = split_pair(jax.nn.gelu(sums[pair + 2, :, 0:128]))
        raised = dot(high, spread_ref[...]) + dot(low, spread_ref[...])
        for x in (2 * pair, 2 * pair + 1):
            joined = jnp.concatenate([fine[x] + raised, cells_ref[rows_of(x), :]], axis=0)
            high, low = split_pair(joined)
            value = dot(point_high, high) + dot(point_high, low) + dot(point_low, high)
            base[rows_of(x), :] = value + bias_ref[...]
    for copy in copies:
        copy.wait()
    load_weight.wait()
    lane = lax.broadcasted_iota(jnp.int32, (channels, lanes), 1)
    sign = jnp.where(lane < half, 1.0, -1.0).astype(jnp.float32)
    group = lane // KZ
    row_8 = lax.broadcasted_iota(jnp.int32, (groups, lanes), 0)
    diagonal = lax.rem(row_8 - lax.broadcasted_iota(jnp.int32, (groups, lanes), 1) // KZ + groups, groups)

    def spread(values, index):
        picked = jnp.where(group == index, values, 0.0)
        shift = KZ
        while shift < lanes:
            picked = picked + pltpu.roll(picked, shift, 1)
            shift *= 2
        return picked

    def along_x(own, others, rows, place):
        first = jnp.zeros((channels, lanes), jnp.float32)
        second = jnp.zeros((channels, lanes), jnp.float32)
        for step in range(groups_x):
            base = lax.rem(mx - step + groups_x, groups_x) * rows
            for row in range(rows):
                position = place(base + row)
                block = pl.ds(row * channels, channels)
                values = own[block, :] if step == 0 else others[step, block, :]
                first = first + values * table_x[position]
                second = second + values * table_x[KX * total_x + position]
        return first, pltpu.roll(second, half, 1) * sign

    def one_mode(j, carry):
        first, second = along_x(line, line_in, cells_x, lambda x: (mx * rows_x + j) * total_x + x)
        modes = first + second
        tiles = channels * KZ // lanes
        rows = [jnp.zeros((groups, lanes), jnp.float32) for _ in range(tiles)]
        for k in range(rows_y):
            real, imag = spread(modes, k), spread(modes, rows_y + k)
            for tile in range(tiles):
                columns = pl.ds(tile * lanes, lanes)
                w_real = weight[j, k, 0, :, columns]
                w_imag = weight[j, k, 1, :, columns]
                out_real = jnp.sum(real * w_real - imag * w_imag, axis=0, keepdims=True)
                out_imag = jnp.sum(real * w_imag + imag * w_real, axis=0, keepdims=True)
                rows[tile] = jnp.where(row_8 == k, out_real, rows[tile])
                rows[tile] = jnp.where(row_8 == rows_y + k, out_imag, rows[tile])
        for tile in range(tiles):
            turned = jnp.where(diagonal == 0, rows[tile], 0.0)
            for d in range(1, groups):
                moved = pltpu.roll(pltpu.roll(rows[tile], d, 0), lanes - KZ * d, 1)
                turned = jnp.where(diagonal == d, moved, turned)
            start = pl.multiple_of(j * channels + tile * groups, groups)
            mixed[pl.ds(start, groups), :] = turned
        return carry

    lax.fori_loop(0, rows_x, one_mode, 0)
    copies = [
        send(2, step, mixed, mixed_in.at[step], (lax.rem(mx + step, groups_x), my))
        for step in range(1, groups_x)
    ]
    for copy in copies:
        copy.wait()

    def one_line(j, carry):
        first, second = along_x(mixed, mixed_in, rows_x, lambda k: k * total_x + mx * cells_x + j)
        back[pl.ds(pl.multiple_of(j * channels, channels), channels), :] = first - second
        return carry

    lax.fori_loop(0, cells_x, one_line, 0)
    copies = [
        send(3, step, back, back_in.at[step], (mx, lax.rem(my + step, groups_y)))
        for step in range(1, groups_y)
    ]
    result = None
    for step in range(groups_y):
        if step:
            copies[step - 1].wait()
        values = back_in[step] if step else back[...]
        peer = lax.rem(my - step + groups_y, groups_y)
        turn = rotation[my * groups_y + peer]
        values = values * turn[0:1] - pltpu.roll(values, half, 1) * turn[1:2]
        term = dot_split(values, inv_high[peer], inv_low[peer])
        result = term if result is None else result + term
    out_ref[...] = jax.nn.gelu(result + base[...])


def stacked(weight):
    taps, outs, ins = weight.shape
    return weight.reshape(3, 9, outs, ins).transpose(0, 2, 1, 3).reshape(3 * outs, 9 * ins)


def pooling(cells_y):
    cells = np.arange(cells_y * NZ)
    short = NZ // 2
    place = short + cells // NZ // 2 * short + cells % NZ // 2
    hit = place[:, None] == np.arange(128)[None, :]
    pool = jnp.asarray((hit * 0.125).astype(jnp.bfloat16))
    return pool, jnp.asarray(hit.T.astype(np.float32).astype(jnp.bfloat16))


def layer(
    cells, spectral_weight, conv_fine, conv_coarse, conv_mix, linear_weight, bias_vector, cells_y
):
    cells_x, channels, plane = cells.shape
    rows_x, rows_y = spectral_weight.shape[:2]
    groups_x, groups_y = lax.axis_size("gx"), lax.axis_size("gy")
    lanes = 2 * rows_y * KZ
    tables = spectral_tables(groups_x, groups_y, cells_x, cells_y, rows_y)
    slab_x, slab_k = (cells_x * channels, lanes), (rows_x * channels, lanes)
    f32 = jnp.float32
    vmem = pl.BlockSpec(memory_space=pltpu.VMEM)
    return pl.pallas_call(
        functools.partial(
            spectral_kernel, groups_x, groups_y, cells_x, rows_x, rows_y, channels
        ),
        out_shape=jax.ShapeDtypeStruct((cells_x * channels, plane), f32),
        in_specs=[vmem] * 6
        + [pl.BlockSpec(memory_space=pltpu.SMEM), pl.BlockSpec(memory_space=pl.ANY)]
        + [vmem] * 6,
        out_specs=vmem,
        scratch_shapes=[
            pltpu.VMEM((groups_y, *slab_x), f32),
            pltpu.VMEM((groups_y, *slab_x), f32),
            pltpu.VMEM(slab_x, f32),
            pltpu.VMEM((groups_x, *slab_x), f32),
            pltpu.VMEM(slab_k, f32),
            pltpu.VMEM((groups_x, *slab_k), f32),
            pltpu.VMEM(slab_x, f32),
            pltpu.VMEM((groups_y, *slab_x), f32),
            pltpu.VMEM(spectral_weight.shape, f32),
            pltpu.SemaphoreType.DMA((4, max(groups_x, groups_y))),
            pltpu.SemaphoreType.DMA((4, max(groups_x, groups_y))),
            pltpu.SemaphoreType.DMA,
            pltpu.VMEM((2, cells_x * NZ // 128, channels, 128), f32),
            pltpu.VMEM((2, cells_x * NZ // 128, channels, 128), f32),
            pltpu.VMEM((2, channels, plane), f32),
            pltpu.VMEM((2, 2, channels, 128), f32),
            pltpu.VMEM((cells_x + 2, channels, plane + 256), f32),
            pltpu.VMEM((9 * channels, plane), jnp.bfloat16),
            pltpu.VMEM((9 * channels, plane), jnp.bfloat16),
            pltpu.VMEM((cells_x + 4, channels, plane), f32),
            pltpu.VMEM((cells_x, channels, plane), f32),
            pltpu.VMEM((cells_x // 2, channels, 128), f32),
            pltpu.VMEM((channels, 128), f32),
            pltpu.VMEM((2, channels, 128), f32),
            pltpu.VMEM((2, channels, 128), f32),
            pltpu.VMEM((2, 2, channels, 128), f32),
            pltpu.VMEM((cells_x // 2 + 2, channels, 128), f32),
            pltpu.VMEM((cells_x * channels, plane), f32),
            pltpu.SemaphoreType.DMA((2, 8)),
            pltpu.SemaphoreType.DMA((2, 8)),
        ],
        compiler_params=pltpu.CompilerParams(
            collective_id=0, has_side_effects=True, vmem_limit_bytes=32 * 1024 * 1024
        ),
    )(
        cells.reshape(cells_x * channels, plane), *tables, spectral_weight,
        stacked(conv_fine), stacked(conv_coarse),
        jnp.concatenate([conv_mix, linear_weight], axis=1), bias_vector[:, None],
        *pooling(cells_y),
    )


def spectral_general(volume, spectral_weight):
    channels, cells_x, cells_y, _ = volume.shape
    total_x = cells_x * lax.axis_size("gx")
    total_y = cells_y * lax.axis_size("gy")
    merged = channels * KZ
    depth_modes = jnp.arange(KZ, dtype=jnp.int32)
    depth_cells = jnp.arange(NZ, dtype=jnp.int32)
    depth_angles = (depth_cells[:, None] * depth_modes[None, :] % NZ).astype(jnp.float32) * (
        2.0 * math.pi / NZ
    )
    depth_forward = jnp.stack([jnp.cos(depth_angles), -jnp.sin(depth_angles)], axis=1)
    along_z = jnp.einsum("cxyz,zqk->xyqck", volume, depth_forward, precision=exact_precision)
    along_z = along_z.reshape(cells_x, cells_y, 2, merged)
    table_x = forward_table(KX, total_x, lax.axis_index("gx") * cells_x, cells_x)
    table_y = forward_table(KY, total_y, lax.axis_index("gy") * cells_y, cells_y)
    inverse_x = jnp.transpose(table_x, (2, 3, 0, 1))
    inverse_y = jnp.transpose(table_y, (2, 3, 0, 1))
    part_x = jnp.einsum("kpxq,xyqm->kypm", table_x, along_z, precision=exact_precision)
    summed_x = lax.psum_scatter(part_x, "gx", scatter_dimension=0, tiled=True)
    partials = jnp.einsum("jpyq,kyqm->kjpm", table_y, summed_x, precision=exact_precision)
    owned_modes = lax.psum_scatter(partials, "gy", scatter_dimension=1, tiled=True)
    mixed_modes = mix_modes(owned_modes, spectral_weight, channels)
    whole_y = lax.all_gather(mixed_modes, "gy", axis=1, tiled=True)
    back_y = jnp.einsum("ypjq,kjqm->kypm", inverse_y, whole_y, precision=exact_precision)
    whole_x = lax.all_gather(back_y, "gx", axis=0, tiled=True)
    back_x = jnp.einsum("xpkq,kyqm->xypm", inverse_x, whole_x, precision=exact_precision)
    weights_z = jnp.where(depth_modes == 0, 1.0, 2.0).astype(jnp.float32) / (total_x * total_y * NZ)
    inverse_angles = jnp.transpose(depth_angles)
    depth_inverse = jnp.stack(
        [
            weights_z[:, None] * jnp.cos(inverse_angles),
            -weights_z[:, None] * jnp.sin(inverse_angles),
        ],
        axis=0,
    )
    fourier = jnp.einsum(
        "xyqck,qkz->cxyz",
        back_x.reshape(cells_x, cells_y, 2, channels, KZ),
        depth_inverse,
        precision=exact_precision,
    )
    return fourier.reshape(channels, cells_x, cells_y * NZ)


def per_device(
    state_field, spectral_weight, conv_fine, conv_coarse, conv_mix, linear_weight, bias_vector
):
    channels, cells_x, plane = state_field.shape
    cells_y = plane // NZ
    rows_y = spectral_weight.shape[1]
    if (
        2 * rows_y * KZ == 128
        and 2 * rows_y == 8
        and channels * KZ % 128 == 0
        and plane % 128 == 0
        and cells_x % (128 // NZ) == 0
        and cells_x * NZ // 2 == 128
        and cells_x == cells_y
        and min(lax.axis_size("gx"), lax.axis_size("gy")) > 1
    ):
        out = layer(
            jnp.transpose(state_field, (1, 0, 2)), spectral_weight, conv_fine, conv_coarse,
            conv_mix, linear_weight, bias_vector, cells_y,
        )
        return jnp.transpose(out.reshape(cells_x, channels, plane), (1, 0, 2))
    volume = state_field.reshape(channels, cells_x, cells_y, NZ)
    padded = extended(volume, (("gx", 1), ("gy", 2)), 1)
    fine_level = jax.nn.gelu(conv_merged(padded, conv_fine, cells_x, cells_y, NZ))
    pooled = fine_level.reshape(channels, cells_x // 2, 2, cells_y // 2, 2, NZ // 2, 2).mean(
        axis=(2, 4, 6)
    )
    coarse_padded = extended(pooled, (("gx", 1), ("gy", 2)), 1)
    coarse = jax.nn.gelu(
        conv_merged(coarse_padded, conv_coarse, cells_x // 2, cells_y // 2, NZ // 2)
    )
    coarse = coarse.reshape(channels, cells_x // 2, 1, cells_y // 2, 1, NZ // 2, 1)
    spread = jnp.broadcast_to(coarse, (channels, cells_x // 2, 2, cells_y // 2, 2, NZ // 2, 2))
    joined = fine_level + spread.reshape(channels, cells_x, cells_y * NZ)
    unet_branch = jnp.einsum("oi,ixw->oxw", conv_mix, joined, precision=exact_precision)
    pointwise = jnp.einsum("oi,ixw->oxw", linear_weight, state_field, precision=exact_precision)
    fourier = spectral_general(volume, spectral_weight)
    summed = fourier + unet_branch + pointwise + bias_vector[:, None, None]
    return jax.nn.gelu(summed)


def solution(mesh):
    placed = (P(None, "gx", "gy"), P("gx", "gy", None, None, None), P(), P(), P(), P(), P())
    return jax.shard_map(
        per_device, mesh=mesh, in_specs=placed, out_specs=P(None, "gx", "gy"), check_vma=False
    )
```

```python
import functools
import math

import jax
import jax.numpy as jnp
import numpy as np
from jax import lax
from jax.experimental import pallas as pl
from jax.experimental.pallas import tpu as pltpu
from jax.sharding import PartitionSpec as P

KX = 32
KY = 32
KZ = 16
NZ = 32


exact_precision = lax.Precision.HIGH


def extended(cells, sides, width):
    for axis, dim in sides:
        count = lax.axis_size(axis)
        ends = count - 1
        head = lax.slice_in_dim(cells, 0, width, axis=dim)
        tail = lax.slice_in_dim(cells, cells.shape[dim] - width, cells.shape[dim], axis=dim)
        cells = jnp.concatenate(
            [
                lax.ppermute(tail, axis, [(i, (i + 1) % count) for i in range(ends)]),
                cells,
                lax.ppermute(head, axis, [((i + 1) % count, i) for i in range(ends)]),
            ],
            axis=dim,
        )
    return cells


def mode_frequency(count, length):
    indices = jnp.arange(count, dtype=jnp.int32)
    return jnp.where(indices < count // 2, indices, indices - count + length)


def forward_table(count, length, start, cells):
    frequency = mode_frequency(count, length)
    places = start + jnp.arange(cells, dtype=jnp.int32)
    phase = frequency[:, None] * places[None, :] % length
    angles = phase.astype(jnp.float32) * (2.0 * math.pi / length)
    cosines = jnp.cos(angles)
    sines = jnp.sin(angles)
    upper_rows = jnp.stack([cosines, sines], axis=-1)
    lower_rows = jnp.stack([-sines, cosines], axis=-1)
    return jnp.stack([upper_rows, lower_rows], axis=1)


def conv_merged(padded, weight, cells_x, cells_y, depth):
    channels = padded.shape[0]
    flat = padded.reshape(channels, cells_x + 2, (cells_y + 2) * depth)
    flat = jnp.pad(flat, ((0, 0), (0, 0), (1, 1)))
    width = cells_y * depth
    positions = jnp.arange(width, dtype=jnp.int32) % depth
    lower_keep = (positions > 0).astype(jnp.float32)
    upper_keep = (positions < depth - 1).astype(jnp.float32)
    accumulated = jnp.zeros((channels, cells_x, width), jnp.float32)
    for offset in range(27):
        shift_x, shift_y, shift_z = (offset // 9, offset // 3 % 3, offset % 3)
        start = shift_y * depth + shift_z
        window = flat[:, shift_x : shift_x + cells_x, start : start + width]
        term = jnp.einsum("oi,ixw->oxw", weight[offset], window, precision=exact_precision)
        if shift_z == 0:
            term = term * lower_keep
        elif shift_z == 2:
            term = term * upper_keep
        accumulated = accumulated + term
    return accumulated


def contract(values, kernel):
    return jnp.einsum("xyiz,xyioz->xyoz", values, kernel, precision=exact_precision)


def mix_modes(owned_modes, spectral_weight, channels):
    rows_x, rows_y = (owned_modes.shape[0], owned_modes.shape[1])
    values = owned_modes.reshape(rows_x, rows_y, 2, channels, KZ)
    kernel = spectral_weight.reshape(rows_x, rows_y, 2, channels, channels, KZ)
    real_part = contract(values[:, :, 0], kernel[:, :, 0]) - contract(
        values[:, :, 1], kernel[:, :, 1]
    )
    imag_part = contract(values[:, :, 0], kernel[:, :, 1]) + contract(
        values[:, :, 1], kernel[:, :, 0]
    )
    return jnp.stack([real_part, imag_part], axis=2).reshape(rows_x, rows_y, 2, channels * KZ)


MESH = pl.DeviceIdType.MESH


def split_pair(values):
    high = values.astype(jnp.bfloat16)
    return high, (values - high.astype(jnp.float32)).astype(jnp.bfloat16)


def dot_split(left, high, low):
    left_high, left_low = split_pair(left)
    dot = functools.partial(jnp.dot, preferred_element_type=jnp.float32)
    return dot(left_high, high) + dot(left_high, low) + dot(left_low, high)


def host_pair(values):
    high = values.astype(np.float32).astype(jnp.bfloat16)
    low = (values - high.astype(np.float64)).astype(np.float32).astype(jnp.bfloat16)
    return jnp.asarray(high), jnp.asarray(low)


def host_frequency(count, length):
    indices = np.arange(count)
    return np.where(indices < count // 2, indices, indices - count + length)


def spectral_tables(groups_x, groups_y, cells_x, cells_y, rows_y):
    total_x, total_y = groups_x * cells_x, groups_y * cells_y
    fy = host_frequency(KY, total_y)
    places = np.arange(cells_y)
    kz = np.arange(KZ)
    zs = np.arange(NZ)
    turn_y = places[:, None] * fy[None, :] % total_y / total_y
    turn_z = zs[:, None] * kz[None, :] % NZ / NZ
    angle = 2 * np.pi * (turn_y[:, None, :, None] + turn_z[None, :, None, :])
    table = np.stack([np.cos(angle), -np.sin(angle)], axis=2)
    table = table.reshape(cells_y * NZ, 2, groups_y, rows_y, KZ).transpose(2, 0, 1, 3, 4)
    table = table.reshape(groups_y, cells_y * NZ, 2 * rows_y * KZ)
    scale = np.tile(np.where(kz == 0, 1.0, 2.0) / (total_x * total_y * NZ), 2 * rows_y)
    inverse = (table * scale).transpose(0, 2, 1)
    starts = np.arange(groups_y) * cells_y
    phase = 2 * np.pi * (starts[:, None] * fy[None, :] % total_y) / total_y
    phase = np.broadcast_to(phase.reshape(-1, 1, rows_y, 1), (groups_y**2, 2, rows_y, KZ))
    signs = np.array([1.0, -1.0]).reshape(1, 2, 1, 1)
    rotation = np.stack([np.cos(phase), signs * np.sin(phase)], axis=1)
    rotation = rotation.reshape(groups_y**2, 2, 2 * rows_y * KZ).astype(np.float32)
    fx = host_frequency(KX, total_x)
    angle_x = 2 * np.pi * (fx[:, None] * np.arange(total_x)[None, :] % total_x) / total_x
    table_x = np.stack([np.cos(angle_x), np.sin(angle_x)]).reshape(-1).astype(np.float32)
    return (*host_pair(table), *host_pair(inverse), jnp.asarray(rotation), jnp.asarray(table_x))


def lane_group(shape, axis, width):
    return lax.broadcasted_iota(jnp.int32, shape, axis) // width


def spectral_kernel(
    groups_x, groups_y, cells_x, rows_x, rows_y, channels,
    cells_ref, fwd_high, fwd_low, inv_high, inv_low, rotation, table_x, weight_hbm,
    fine_ref, coarse_ref, point_ref, bias_ref, pool_ref, spread_ref,
    out_ref,
    field_in, parts, lines, lines_in, mixed, mixed_in, back, back_in, ready, ready_in, weight,
    send_sem, recv_sem, relay_send, relay_recv, weight_sem,
    edges, edges_in, planes_in, corners_in, padded, stack_high, stack_low, sums, fine,
    pooled, rim, rim_in, pooled_in, rim_corners_in, coarse_padded, base,
    halo_send, halo_recv,
):
    mx, my = lax.axis_index("gx"), lax.axis_index("gy")
    lanes = 2 * rows_y * KZ
    groups = 2 * rows_y
    total_x = groups_x * cells_x
    load_weight = pltpu.make_async_copy(weight_hbm, weight, weight_sem)
    load_weight.start()
    barrier = pltpu.get_barrier_semaphore()
    for step in range(1, groups_y):
        pl.semaphore_signal(
            barrier, inc=1, device_id=(mx, lax.rem(my + step, groups_y)), device_id_type=MESH
        )
    for step in range(1, groups_x):
        pl.semaphore_signal(
            barrier, inc=1, device_id=(lax.rem(mx + step, groups_x), my), device_id_type=MESH
        )
    up_x, down_x = lax.rem(mx + 1, groups_x), lax.rem(mx + groups_x - 1, groups_x)
    up_y, down_y = lax.rem(my + 1, groups_y), lax.rem(my + groups_y - 1, groups_y)
    sides_x, sides_y = (down_x, up_x), (down_y, up_y)
    for to_x in sides_x:
        for to_y in sides_y:
            pl.semaphore_signal(barrier, inc=1, device_id=(to_x, to_y), device_id_type=MESH)
    pl.semaphore_wait(barrier, groups_x + groups_y + 2)

    def halo(phase, index, source, target, device):
        copy = pltpu.make_async_remote_copy(
            src_ref=source, dst_ref=target,
            send_sem=halo_send.at[phase, index], recv_sem=halo_recv.at[phase, index],
            device_id=device, device_id_type=MESH,
        )
        copy.start()
        return copy

    def rows_of(plane):
        return pl.ds(plane * channels, channels)

    def send(phase, step, source, target, device):
        copy = pltpu.make_async_remote_copy(
            src_ref=source, dst_ref=target,
            send_sem=send_sem.at[phase, step], recv_sem=recv_sem.at[phase, step],
            device_id=device, device_id_type=MESH,
        )
        copy.start()
        return copy

    def aligned(row):
        return pl.ds(pl.multiple_of(row * channels, channels), channels)

    fields = []
    for step in range(1, groups_y):
        peer = lax.rem(my + step, groups_y)
        fields.append(
            send(0, step, cells_ref.at[aligned(peer), :], field_in.at[step], (mx, peer))
        )
    lane_full = lax.broadcasted_iota(jnp.int32, (channels, 128), 1)
    plane_lanes = cells_ref.shape[1]
    per_tile = 128 // NZ
    last_tile = cells_x // per_tile - 1
    for tile in range(cells_x // per_tile):
        first = jnp.zeros((channels, 128), jnp.float32)
        last = jnp.zeros((channels, 128), jnp.float32)
        for slot in range(per_tile):
            rows = rows_of(tile * per_tile + slot)
            here = lane_full // NZ == slot
            head = cells_ref[rows, 0:128]
            tail = cells_ref[rows, plane_lanes - 128 : plane_lanes]
            first = jnp.where(here, pltpu.roll(head, slot * NZ, 1), first)
            last = jnp.where(here, pltpu.roll(tail, (slot * NZ + NZ) % 128, 1), last)
        edges[0, tile] = first
        edges[1, tile] = last
    halos = []
    for side in range(2):
        edge_plane = cells_ref.at[rows_of(side * (cells_x - 1)), :]
        halos.append(halo(0, side, edge_plane, planes_in.at[1 - side], (sides_x[side], my)))
        halos.append(halo(0, 2 + side, edges.at[side], edges_in.at[1 - side], (mx, sides_y[side])))
        for other in range(2):
            halos.append(
                halo(
                    0, 4 + 2 * side + other, edges.at[other, side * last_tile],
                    corners_in.at[1 - side, 1 - other], (sides_x[side], sides_y[other]),
                )
            )

    half = lanes // 2
    dot = functools.partial(jnp.dot, preferred_element_type=jnp.float32)
    for copy in fields:
        copy.wait()
    sources = [lax.rem(my - step + groups_y, groups_y) for step in range(groups_y)]
    stack = [cells_ref[aligned(my), :]] + [field_in[step] for step in range(1, groups_y)]
    left_high, left_low = split_pair(jnp.concatenate(stack, axis=0))
    copies = [None] * groups_y
    for step in list(range(1, groups_y)) + [0]:
        peer = lax.rem(my + step, groups_y)
        high, low = fwd_high[peer], fwd_low[peer]
        part = dot(left_high, high) + dot(left_high, low) + dot(left_low, high)
        first = jnp.zeros((channels, lanes), jnp.float32)
        second = jnp.zeros((channels, lanes), jnp.float32)
        for place, source in enumerate(sources):
            turn = rotation[source * groups_y + peer]
            piece = part[place * channels : (place + 1) * channels]
            first = first + piece * turn[0:1]
            second = second + piece * turn[1:2]
        slab = first - pltpu.roll(second, half, 1)
        if step:
            parts[step] = slab
            copies[step] = send(1, step, parts.at[step], lines.at[step], (mx, peer))
        else:
            lines[0] = slab
    relays = []
    for step in range(groups_y):
        if step:
            copies[step].wait()
        for hop in range(1, groups_x):
            relay = pltpu.make_async_remote_copy(
                src_ref=lines.at[step], dst_ref=lines_in.at[hop, step],
                send_sem=relay_send.at[hop, step], recv_sem=relay_recv.at[hop, step],
                device_id=(lax.rem(mx + hop, groups_x), my), device_id_type=MESH,
            )
            relay.start()
            relays.append(relay)
    f32 = jnp.float32
    at_x = ((mx > 0).astype(f32), (mx < groups_x - 1).astype(f32))
    at_y = ((my > 0).astype(f32), (my < groups_y - 1).astype(f32))
    for copy in halos:
        copy.wait()

    def fill(plane, main, left, right, left_slot, right_slot, scale):
        padded[plane, :, 0:128] = (
            pltpu.roll(left, (128 - NZ - left_slot * NZ) % 128, 1) * (at_y[0] * scale)
        )
        padded[plane, :, 128 : 128 + plane_lanes] = main * scale
        padded[plane, :, 128 + plane_lanes : 256 + plane_lanes] = (
            pltpu.roll(right, (128 - right_slot * NZ) % 128, 1) * (at_y[1] * scale)
        )

    for x in range(cells_x):
        tile, slot = x // per_tile, x % per_tile
        fill(x + 1, cells_ref[rows_of(x), :], edges_in[0, tile], edges_in[1, tile], slot, slot, 1.0)
    end = per_tile - 1
    fill(0, planes_in[0], corners_in[0, 0], corners_in[0, 1], end, end, at_x[0])
    fill(cells_x + 1, planes_in[1], corners_in[1, 0], corners_in[1, 1], 0, 0, at_x[1])

    def convolve(source, kernel, count, width, start, depth):
        kernel_high, kernel_low = split_pair(kernel)
        total_lanes = source.shape[2]
        depths = lax.broadcasted_iota(jnp.int32, (channels, width), 1) % depth
        for slot in range(count + 4):
            sums[slot, :, 0:width] = jnp.zeros((channels, width), f32)

        def one_plane(plane, carry):
            values = source[plane]
            for tap in range(9):
                shift_y, shift_z = tap // 3 - 1, tap % 3 - 1
                moved = pltpu.roll(values, (-shift_y * depth - shift_z) % total_lanes, 1)
                moved = moved[:, start : start + width]
                if shift_z == -1:
                    moved = jnp.where(depths > 0, moved, 0.0)
                elif shift_z == 1:
                    moved = jnp.where(depths < depth - 1, moved, 0.0)
                high, low = split_pair(moved)
                stack_high[tap * channels : (tap + 1) * channels, 0:width] = high
                stack_low[tap * channels : (tap + 1) * channels, 0:width] = low
            high, low = stack_high[:, 0:width], stack_low[:, 0:width]
            term = dot(kernel_high, high) + dot(kernel_high, low) + dot(kernel_low, high)
            for shift_x in range(3):
                piece = term[shift_x * channels : (shift_x + 1) * channels]
                slot = plane - shift_x + 2
                sums[slot, :, 0:width] = sums[slot, :, 0:width] + piece
            return carry

        lax.fori_loop(0, count + 2, one_plane, 0)

    convolve(padded, fine_ref[...], cells_x, plane_lanes, 128, NZ)
    pairs = cells_x // 2
    short = NZ // 2
    for x in range(cells_x):
        fine[x] = jax.nn.gelu(sums[x + 2])
    for pair in range(pairs):
        high, low = split_pair(fine[2 * pair] + fine[2 * pair + 1])
        pooled[pair] = dot(high, pool_ref[...]) + dot(low, pool_ref[...])
    packed = jnp.zeros((channels, 128), f32)
    for pair in range(pairs):
        values = pooled[pair]
        slot = lane_full // short
        packed = jnp.where(slot == pair, pltpu.roll(values, (pair * short - short) % 128, 1), packed)
        packed = jnp.where(slot == pairs + pair, pltpu.roll(values, pair * short, 1), packed)
    rim[...] = packed
    rims = []
    for side in range(2):
        rims.append(
            halo(1, side, pooled.at[side * (pairs - 1)], pooled_in.at[1 - side], (sides_x[side], my))
        )
        rims.append(halo(1, 2 + side, rim, rim_in.at[1 - side], (mx, sides_y[side])))
        for other in range(2):
            rims.append(
                halo(
                    1, 4 + 2 * side + other, rim, rim_corners_in.at[1 - side, 1 - other],
                    (sides_x[side], sides_y[other]),
                )
            )
    for copy in relays:
        copy.wait()
    load_weight.wait()
    lane = lax.broadcasted_iota(jnp.int32, (channels, lanes), 1)
    sign = jnp.where(lane < half, 1.0, -1.0).astype(jnp.float32)
    group = lane // KZ
    row_8 = lax.broadcasted_iota(jnp.int32, (groups, lanes), 0)
    diagonal = lax.rem(row_8 - lax.broadcasted_iota(jnp.int32, (groups, lanes), 1) // KZ + groups, groups)

    def spread(values, index):
        picked = jnp.where(group == index, values, 0.0)
        shift = KZ
        while shift < lanes:
            picked = picked + pltpu.roll(picked, shift, 1)
            shift *= 2
        return picked

    def along_x(terms):
        first = jnp.zeros((channels, lanes), jnp.float32)
        second = jnp.zeros((channels, lanes), jnp.float32)
        for values, position in terms:
            first = first + values * table_x[position]
            second = second + values * table_x[KX * total_x + position]
        return first, pltpu.roll(second, half, 1) * sign

    def shifted(step):
        return lax.rem(mx - step + groups_x, groups_x)

    def one_mode(j, carry):
        first, second = along_x(
            (
                lines[step] if hop == 0 else lines_in[hop, step],
                (mx * rows_x + j) * total_x + shifted(hop) * cells_x + sources[step],
            )
            for hop in range(groups_x)
            for step in range(groups_y)
        )
        modes = first + second
        tiles = channels * KZ // lanes
        rows = [jnp.zeros((groups, lanes), jnp.float32) for _ in range(tiles)]
        for k in range(rows_y):
            real, imag = spread(modes, k), spread(modes, rows_y + k)
            for tile in range(tiles):
                columns = pl.ds(tile * lanes, lanes)
                w_real = weight[j, k, 0, :, columns]
                w_imag = weight[j, k, 1, :, columns]
                out_real = jnp.sum(real * w_real - imag * w_imag, axis=0, keepdims=True)
                out_imag = jnp.sum(real * w_imag + imag * w_real, axis=0, keepdims=True)
                rows[tile] = jnp.where(row_8 == k, out_real, rows[tile])
                rows[tile] = jnp.where(row_8 == rows_y + k, out_imag, rows[tile])
        for tile in range(tiles):
            turned = jnp.where(diagonal == 0, rows[tile], 0.0)
            for d in range(1, groups):
                moved = pltpu.roll(pltpu.roll(rows[tile], d, 0), lanes - KZ * d, 1)
                turned = jnp.where(diagonal == d, moved, turned)
            start = pl.multiple_of(j * channels + tile * groups, groups)
            mixed[pl.ds(start, groups), :] = turned
        return carry

    lax.fori_loop(0, rows_x, one_mode, 0)
    copies = [
        send(2, step, mixed, mixed_in.at[step], (lax.rem(mx + step, groups_x), my))
        for step in range(1, groups_x)
    ]
    for copy in rims:
        copy.wait()
    inner = short * (pairs + 1)

    def fill_coarse(plane, main, left, right, slot, scale):
        before = pltpu.roll(left, (128 - (pairs + slot) * short) % 128, 1) * at_y[0]
        after = pltpu.roll(right, (inner - slot * short) % 128, 1) * at_y[1]
        values = jnp.where(lane_full < short, before, main)
        values = jnp.where(lane_full // short == pairs + 1, after, values)
        coarse_padded[plane] = values * scale

    for pair in range(pairs):
        fill_coarse(pair + 1, pooled[pair], rim_in[0], rim_in[1], pair, 1.0)
    fill_coarse(0, pooled_in[0], rim_corners_in[0, 0], rim_corners_in[0, 1], pairs - 1, at_x[0])
    fill_coarse(pairs + 1, pooled_in[1], rim_corners_in[1, 0], rim_corners_in[1, 1], 0, at_x[1])
    convolve(coarse_padded, coarse_ref[...], pairs, 128, 0, short)
    point_high, point_low = split_pair(point_ref[...])
    for pair in range(pairs):
        high, low = split_pair(jax.nn.gelu(sums[pair + 2, :, 0:128]))
        raised = dot(high, spread_ref[...]) + dot(low, spread_ref[...])
        for x in (2 * pair, 2 * pair + 1):
            joined = jnp.concatenate([fine[x] + raised, cells_ref[rows_of(x), :]], axis=0)
            high, low = split_pair(joined)
            value = dot(point_high, high) + dot(point_high, low) + dot(point_low, high)
            base[rows_of(x), :] = value + bias_ref[...]
    for copy in copies:
        copy.wait()

    def one_line(step, carry):
        place = mx * cells_x + lax.rem(my + step, groups_y)
        first, second = along_x(
            (
                mixed[rows_of(row), :] if hop == 0 else mixed_in[hop, rows_of(row), :],
                (shifted(hop) * rows_x + row) * total_x + place,
            )
            for hop in range(groups_x)
            for row in range(rows_x)
        )
        back[step] = first - second
        return carry

    lax.fori_loop(0, groups_y, one_line, 0)
    copies = [None] + [
        send(3, step, back.at[step], back_in.at[step], (mx, lax.rem(my + step, groups_y)))
        for step in range(1, groups_y)
    ]
    result = None
    for step in range(groups_y):
        if step:
            copies[step].wait()
        values = back_in[step] if step else back[0]
        peer = sources[step]
        rolled = pltpu.roll(values, half, 1)
        turned = []
        for tile in range(groups_y):
            turn = rotation[lax.rem(my + tile, groups_y) * groups_y + peer]
            turned.append(values * turn[0:1] - rolled * turn[1:2])
        term = dot_split(jnp.concatenate(turned, axis=0), inv_high[peer], inv_low[peer])
        result = term if result is None else result + term
    for step in range(groups_y):
        ready[step] = result[step * channels : (step + 1) * channels]
    copies = [None] + [
        send(4, step, ready.at[step], ready_in.at[step], (mx, lax.rem(my + step, groups_y)))
        for step in range(1, groups_y)
    ]
    for step in range(groups_y):
        if step:
            copies[step].wait()
        values = ready_in[step] if step else ready[0]
        rows = aligned(sources[step])
        out_ref[rows, :] = jax.nn.gelu(values + base[rows, :])


def stacked(weight):
    taps, outs, ins = weight.shape
    return weight.reshape(3, 9, outs, ins).transpose(0, 2, 1, 3).reshape(3 * outs, 9 * ins)


def pooling(cells_y):
    cells = np.arange(cells_y * NZ)
    short = NZ // 2
    place = short + cells // NZ // 2 * short + cells % NZ // 2
    hit = place[:, None] == np.arange(128)[None, :]
    pool = jnp.asarray((hit * 0.125).astype(jnp.bfloat16))
    return pool, jnp.asarray(hit.T.astype(np.float32).astype(jnp.bfloat16))


def layer(
    cells, spectral_weight, conv_fine, conv_coarse, conv_mix, linear_weight, bias_vector, cells_y
):
    cells_x, channels, plane = cells.shape
    rows_x, rows_y = spectral_weight.shape[:2]
    groups_x, groups_y = lax.axis_size("gx"), lax.axis_size("gy")
    lanes = 2 * rows_y * KZ
    tables = spectral_tables(groups_x, groups_y, cells_x, cells_y, rows_y)
    slab_k = (rows_x * channels, lanes)
    f32 = jnp.float32
    vmem = pl.BlockSpec(memory_space=pltpu.VMEM)
    return pl.pallas_call(
        functools.partial(
            spectral_kernel, groups_x, groups_y, cells_x, rows_x, rows_y, channels
        ),
        out_shape=jax.ShapeDtypeStruct((cells_x * channels, plane), f32),
        in_specs=[vmem] * 6
        + [pl.BlockSpec(memory_space=pltpu.SMEM), pl.BlockSpec(memory_space=pl.ANY)]
        + [vmem] * 6,
        out_specs=vmem,
        scratch_shapes=[
            pltpu.VMEM((groups_y, channels, plane), f32),
            pltpu.VMEM((groups_y, channels, lanes), f32),
            pltpu.VMEM((groups_y, channels, lanes), f32),
            pltpu.VMEM((groups_x, groups_y, channels, lanes), f32),
            pltpu.VMEM(slab_k, f32),
            pltpu.VMEM((groups_x, *slab_k), f32),
            pltpu.VMEM((groups_y, channels, lanes), f32),
            pltpu.VMEM((groups_y, channels, lanes), f32),
            pltpu.VMEM((groups_y, channels, plane), f32),
            pltpu.VMEM((groups_y, channels, plane), f32),
            pltpu.VMEM(spectral_weight.shape, f32),
            pltpu.SemaphoreType.DMA((5, max(groups_x, groups_y))),
            pltpu.SemaphoreType.DMA((5, max(groups_x, groups_y))),
            pltpu.SemaphoreType.DMA((groups_x, groups_y)),
            pltpu.SemaphoreType.DMA((groups_x, groups_y)),
            pltpu.SemaphoreType.DMA,
            pltpu.VMEM((2, cells_x * NZ // 128, channels, 128), f32),
            pltpu.VMEM((2, cells_x * NZ // 128, channels, 128), f32),
            pltpu.VMEM((2, channels, plane), f32),
            pltpu.VMEM((2, 2, channels, 128), f32),
            pltpu.VMEM((cells_x + 2, channels, plane + 256), f32),
            pltpu.VMEM((9 * channels, plane), jnp.bfloat16),
            pltpu.VMEM((9 * channels, plane), jnp.bfloat16),
            pltpu.VMEM((cells_x + 4, channels, plane), f32),
            pltpu.VMEM((cells_x, channels, plane), f32),
            pltpu.VMEM((cells_x // 2, channels, 128), f32),
            pltpu.VMEM((channels, 128), f32),
            pltpu.VMEM((2, channels, 128), f32),
            pltpu.VMEM((2, channels, 128), f32),
            pltpu.VMEM((2, 2, channels, 128), f32),
            pltpu.VMEM((cells_x // 2 + 2, channels, 128), f32),
            pltpu.VMEM((cells_x * channels, plane), f32),
            pltpu.SemaphoreType.DMA((2, 8)),
            pltpu.SemaphoreType.DMA((2, 8)),
        ],
        compiler_params=pltpu.CompilerParams(
            collective_id=0, has_side_effects=True, vmem_limit_bytes=32 * 1024 * 1024
        ),
    )(
        cells.reshape(cells_x * channels, plane), *tables, spectral_weight,
        stacked(conv_fine), stacked(conv_coarse),
        jnp.concatenate([conv_mix, linear_weight], axis=1), bias_vector[:, None],
        *pooling(cells_y),
    )


def spectral_general(volume, spectral_weight):
    channels, cells_x, cells_y, _ = volume.shape
    total_x = cells_x * lax.axis_size("gx")
    total_y = cells_y * lax.axis_size("gy")
    merged = channels * KZ
    depth_modes = jnp.arange(KZ, dtype=jnp.int32)
    depth_cells = jnp.arange(NZ, dtype=jnp.int32)
    depth_angles = (depth_cells[:, None] * depth_modes[None, :] % NZ).astype(jnp.float32) * (
        2.0 * math.pi / NZ
    )
    depth_forward = jnp.stack([jnp.cos(depth_angles), -jnp.sin(depth_angles)], axis=1)
    along_z = jnp.einsum("cxyz,zqk->xyqck", volume, depth_forward, precision=exact_precision)
    along_z = along_z.reshape(cells_x, cells_y, 2, merged)
    table_x = forward_table(KX, total_x, lax.axis_index("gx") * cells_x, cells_x)
    table_y = forward_table(KY, total_y, lax.axis_index("gy") * cells_y, cells_y)
    inverse_x = jnp.transpose(table_x, (2, 3, 0, 1))
    inverse_y = jnp.transpose(table_y, (2, 3, 0, 1))
    part_x = jnp.einsum("kpxq,xyqm->kypm", table_x, along_z, precision=exact_precision)
    summed_x = lax.psum_scatter(part_x, "gx", scatter_dimension=0, tiled=True)
    partials = jnp.einsum("jpyq,kyqm->kjpm", table_y, summed_x, precision=exact_precision)
    owned_modes = lax.psum_scatter(partials, "gy", scatter_dimension=1, tiled=True)
    mixed_modes = mix_modes(owned_modes, spectral_weight, channels)
    whole_y = lax.all_gather(mixed_modes, "gy", axis=1, tiled=True)
    back_y = jnp.einsum("ypjq,kjqm->kypm", inverse_y, whole_y, precision=exact_precision)
    whole_x = lax.all_gather(back_y, "gx", axis=0, tiled=True)
    back_x = jnp.einsum("xpkq,kyqm->xypm", inverse_x, whole_x, precision=exact_precision)
    weights_z = jnp.where(depth_modes == 0, 1.0, 2.0).astype(jnp.float32) / (total_x * total_y * NZ)
    inverse_angles = jnp.transpose(depth_angles)
    depth_inverse = jnp.stack(
        [
            weights_z[:, None] * jnp.cos(inverse_angles),
            -weights_z[:, None] * jnp.sin(inverse_angles),
        ],
        axis=0,
    )
    fourier = jnp.einsum(
        "xyqck,qkz->cxyz",
        back_x.reshape(cells_x, cells_y, 2, channels, KZ),
        depth_inverse,
        precision=exact_precision,
    )
    return fourier.reshape(channels, cells_x, cells_y * NZ)


def per_device(
    state_field, spectral_weight, conv_fine, conv_coarse, conv_mix, linear_weight, bias_vector
):
    channels, cells_x, plane = state_field.shape
    cells_y = plane // NZ
    rows_y = spectral_weight.shape[1]
    if (
        2 * rows_y * KZ == 128
        and 2 * rows_y == 8
        and channels * KZ % 128 == 0
        and plane % 128 == 0
        and cells_x % (128 // NZ) == 0
        and cells_x * NZ // 2 == 128
        and cells_x == cells_y == lax.axis_size("gy")
        and min(lax.axis_size("gx"), lax.axis_size("gy")) > 1
    ):
        out = layer(
            jnp.transpose(state_field, (1, 0, 2)), spectral_weight, conv_fine, conv_coarse,
            conv_mix, linear_weight, bias_vector, cells_y,
        )
        return jnp.transpose(out.reshape(cells_x, channels, plane), (1, 0, 2))
    volume = state_field.reshape(channels, cells_x, cells_y, NZ)
    padded = extended(volume, (("gx", 1), ("gy", 2)), 1)
    fine_level = jax.nn.gelu(conv_merged(padded, conv_fine, cells_x, cells_y, NZ))
    pooled = fine_level.reshape(channels, cells_x // 2, 2, cells_y // 2, 2, NZ // 2, 2).mean(
        axis=(2, 4, 6)
    )
    coarse_padded = extended(pooled, (("gx", 1), ("gy", 2)), 1)
    coarse = jax.nn.gelu(
        conv_merged(coarse_padded, conv_coarse, cells_x // 2, cells_y // 2, NZ // 2)
    )
    coarse = coarse.reshape(channels, cells_x // 2, 1, cells_y // 2, 1, NZ // 2, 1)
    spread = jnp.broadcast_to(coarse, (channels, cells_x // 2, 2, cells_y // 2, 2, NZ // 2, 2))
    joined = fine_level + spread.reshape(channels, cells_x, cells_y * NZ)
    unet_branch = jnp.einsum("oi,ixw->oxw", conv_mix, joined, precision=exact_precision)
    pointwise = jnp.einsum("oi,ixw->oxw", linear_weight, state_field, precision=exact_precision)
    fourier = spectral_general(volume, spectral_weight)
    summed = fourier + unet_branch + pointwise + bias_vector[:, None, None]
    return jax.nn.gelu(summed)


def solution(mesh):
    placed = (P(None, "gx", "gy"), P("gx", "gy", None, None, None), P(), P(), P(), P(), P())
    return jax.shard_map(
        per_device, mesh=mesh, in_specs=placed, out_specs=P(None, "gx", "gy"), check_vma=False
    )
```

```python
import functools
import math

import jax
import jax.numpy as jnp
import numpy as np
from jax import lax
from jax.experimental import pallas as pl
from jax.experimental.pallas import tpu as pltpu
from jax.sharding import PartitionSpec as P

KX = 32
KY = 32
KZ = 16
NZ = 32


exact_precision = lax.Precision.HIGH


def extended(cells, sides, width):
    for axis, dim in sides:
        count = lax.axis_size(axis)
        ends = count - 1
        head = lax.slice_in_dim(cells, 0, width, axis=dim)
        tail = lax.slice_in_dim(cells, cells.shape[dim] - width, cells.shape[dim], axis=dim)
        cells = jnp.concatenate(
            [
                lax.ppermute(tail, axis, [(i, (i + 1) % count) for i in range(ends)]),
                cells,
                lax.ppermute(head, axis, [((i + 1) % count, i) for i in range(ends)]),
            ],
            axis=dim,
        )
    return cells


def mode_frequency(count, length):
    indices = jnp.arange(count, dtype=jnp.int32)
    return jnp.where(indices < count // 2, indices, indices - count + length)


def forward_table(count, length, start, cells):
    frequency = mode_frequency(count, length)
    places = start + jnp.arange(cells, dtype=jnp.int32)
    phase = frequency[:, None] * places[None, :] % length
    angles = phase.astype(jnp.float32) * (2.0 * math.pi / length)
    cosines = jnp.cos(angles)
    sines = jnp.sin(angles)
    upper_rows = jnp.stack([cosines, sines], axis=-1)
    lower_rows = jnp.stack([-sines, cosines], axis=-1)
    return jnp.stack([upper_rows, lower_rows], axis=1)


def conv_merged(padded, weight, cells_x, cells_y, depth):
    channels = padded.shape[0]
    flat = padded.reshape(channels, cells_x + 2, (cells_y + 2) * depth)
    flat = jnp.pad(flat, ((0, 0), (0, 0), (1, 1)))
    width = cells_y * depth
    positions = jnp.arange(width, dtype=jnp.int32) % depth
    lower_keep = (positions > 0).astype(jnp.float32)
    upper_keep = (positions < depth - 1).astype(jnp.float32)
    accumulated = jnp.zeros((channels, cells_x, width), jnp.float32)
    for offset in range(27):
        shift_x, shift_y, shift_z = (offset // 9, offset // 3 % 3, offset % 3)
        start = shift_y * depth + shift_z
        window = flat[:, shift_x : shift_x + cells_x, start : start + width]
        term = jnp.einsum("oi,ixw->oxw", weight[offset], window, precision=exact_precision)
        if shift_z == 0:
            term = term * lower_keep
        elif shift_z == 2:
            term = term * upper_keep
        accumulated = accumulated + term
    return accumulated


def contract(values, kernel):
    return jnp.einsum("xyiz,xyioz->xyoz", values, kernel, precision=exact_precision)


def mix_modes(owned_modes, spectral_weight, channels):
    rows_x, rows_y = (owned_modes.shape[0], owned_modes.shape[1])
    values = owned_modes.reshape(rows_x, rows_y, 2, channels, KZ)
    kernel = spectral_weight.reshape(rows_x, rows_y, 2, channels, channels, KZ)
    real_part = contract(values[:, :, 0], kernel[:, :, 0]) - contract(
        values[:, :, 1], kernel[:, :, 1]
    )
    imag_part = contract(values[:, :, 0], kernel[:, :, 1]) + contract(
        values[:, :, 1], kernel[:, :, 0]
    )
    return jnp.stack([real_part, imag_part], axis=2).reshape(rows_x, rows_y, 2, channels * KZ)


MESH = pl.DeviceIdType.MESH


def split_pair(values):
    high = values.astype(jnp.bfloat16)
    return high, (values - high.astype(jnp.float32)).astype(jnp.bfloat16)


def dot_split(left, high, low):
    left_high, left_low = split_pair(left)
    dot = functools.partial(jnp.dot, preferred_element_type=jnp.float32)
    return dot(left_high, high) + dot(left_high, low) + dot(left_low, high)


def host_pair(values):
    high = values.astype(np.float32).astype(jnp.bfloat16)
    low = (values - high.astype(np.float64)).astype(np.float32).astype(jnp.bfloat16)
    return jnp.asarray(high), jnp.asarray(low)


def host_frequency(count, length):
    indices = np.arange(count)
    return np.where(indices < count // 2, indices, indices - count + length)


def spectral_tables(groups_x, groups_y, cells_x, cells_y, rows_y):
    total_x, total_y = groups_x * cells_x, groups_y * cells_y
    fy = host_frequency(KY, total_y)
    places = np.arange(cells_y)
    kz = np.arange(KZ)
    zs = np.arange(NZ)
    turn_y = places[:, None] * fy[None, :] % total_y / total_y
    turn_z = zs[:, None] * kz[None, :] % NZ / NZ
    angle = 2 * np.pi * (turn_y[:, None, :, None] + turn_z[None, :, None, :])
    table = np.stack([np.cos(angle), -np.sin(angle)], axis=2)
    table = table.reshape(cells_y * NZ, 2, groups_y, rows_y, KZ).transpose(2, 0, 1, 3, 4)
    table = table.reshape(groups_y, cells_y * NZ, 2 * rows_y * KZ)
    scale = np.tile(np.where(kz == 0, 1.0, 2.0) / (total_x * total_y * NZ), 2 * rows_y)
    inverse = (table * scale).transpose(0, 2, 1)
    starts = np.arange(groups_y) * cells_y
    phase = 2 * np.pi * (starts[:, None] * fy[None, :] % total_y) / total_y
    phase = np.broadcast_to(phase.reshape(-1, 1, rows_y, 1), (groups_y**2, 2, rows_y, KZ))
    signs = np.array([1.0, -1.0]).reshape(1, 2, 1, 1)
    rotation = np.stack([np.cos(phase), signs * np.sin(phase)], axis=1)
    rotation = rotation.reshape(groups_y**2, 2, 2 * rows_y * KZ).astype(np.float32)
    fx = host_frequency(KX, total_x)
    angle_x = 2 * np.pi * (fx[:, None] * np.arange(total_x)[None, :] % total_x) / total_x
    table_x = np.stack([np.cos(angle_x), np.sin(angle_x)]).reshape(-1).astype(np.float32)
    return (*host_pair(table), *host_pair(inverse), jnp.asarray(rotation), jnp.asarray(table_x))


def lane_group(shape, axis, width):
    return lax.broadcasted_iota(jnp.int32, shape, axis) // width


def spectral_kernel(
    groups_x, groups_y, cells_x, rows_x, rows_y, channels,
    cells_ref, fwd_high_hbm, fwd_low_hbm, inv_high_hbm, inv_low_hbm, rotation, table_x, weight_hbm,
    fine_ref, coarse_ref, point_ref, bias_ref, pool_ref, spread_ref,
    out_ref,
    field_in, parts, lines, lines_in, mixed, mixed_in, back, back_in, ready, ready_in, weight,
    send_sem, recv_sem, relay_send, relay_recv, weight_sem,
    edges, edges_in, planes_in, corners_in, padded, stack_high, stack_low, sums, fine,
    pooled, rim, rim_in, pooled_in, rim_corners_in, coarse_padded, base,
    halo_send, halo_recv, fwd_high, fwd_low, inv_high, inv_low, table_sem,
    mixed_send, mixed_recv,
):
    mx, my = lax.axis_index("gx"), lax.axis_index("gy")
    lanes = 2 * rows_y * KZ
    groups = 2 * rows_y
    total_x = groups_x * cells_x
    load_weight = pltpu.make_async_copy(weight_hbm, weight, weight_sem)
    loads = [
        pltpu.make_async_copy(source, target, table_sem.at[index])
        for index, (source, target) in enumerate(
            (
                (fwd_high_hbm, fwd_high), (fwd_low_hbm, fwd_low),
                (inv_high_hbm, inv_high), (inv_low_hbm, inv_low),
            )
        )
    ]
    for load in loads:
        load.start()
    load_weight.start()
    barrier = pltpu.get_barrier_semaphore()
    for step in range(1, groups_y):
        pl.semaphore_signal(
            barrier, inc=1, device_id=(mx, lax.rem(my + step, groups_y)), device_id_type=MESH
        )
    for step in range(1, groups_x):
        pl.semaphore_signal(
            barrier, inc=1, device_id=(lax.rem(mx + step, groups_x), my), device_id_type=MESH
        )
    up_x, down_x = lax.rem(mx + 1, groups_x), lax.rem(mx + groups_x - 1, groups_x)
    up_y, down_y = lax.rem(my + 1, groups_y), lax.rem(my + groups_y - 1, groups_y)
    sides_x, sides_y = (down_x, up_x), (down_y, up_y)
    for to_x in sides_x:
        for to_y in sides_y:
            pl.semaphore_signal(barrier, inc=1, device_id=(to_x, to_y), device_id_type=MESH)
    pl.semaphore_wait(barrier, groups_x + groups_y + 2)

    def halo(phase, index, source, target, device):
        copy = pltpu.make_async_remote_copy(
            src_ref=source, dst_ref=target,
            send_sem=halo_send.at[phase, index], recv_sem=halo_recv.at[phase, index],
            device_id=device, device_id_type=MESH,
        )
        copy.start()
        return copy

    def rows_of(plane):
        return pl.ds(plane * channels, channels)

    def send(phase, step, source, target, device):
        copy = pltpu.make_async_remote_copy(
            src_ref=source, dst_ref=target,
            send_sem=send_sem.at[phase, step], recv_sem=recv_sem.at[phase, step],
            device_id=device, device_id_type=MESH,
        )
        copy.start()
        return copy

    def aligned(row):
        return pl.ds(pl.multiple_of(row * channels, channels), channels)

    fields = []
    for step in range(1, groups_y):
        peer = lax.rem(my + step, groups_y)
        fields.append(
            send(0, step, cells_ref.at[aligned(peer), :], field_in.at[step], (mx, peer))
        )
    lane_full = lax.broadcasted_iota(jnp.int32, (channels, 128), 1)
    plane_lanes = cells_ref.shape[1]
    per_tile = 128 // NZ
    last_tile = cells_x // per_tile - 1
    for tile in range(cells_x // per_tile):
        first = jnp.zeros((channels, 128), jnp.float32)
        last = jnp.zeros((channels, 128), jnp.float32)
        for slot in range(per_tile):
            rows = rows_of(tile * per_tile + slot)
            here = lane_full // NZ == slot
            head = cells_ref[rows, 0:128]
            tail = cells_ref[rows, plane_lanes - 128 : plane_lanes]
            first = jnp.where(here, pltpu.roll(head, slot * NZ, 1), first)
            last = jnp.where(here, pltpu.roll(tail, (slot * NZ + NZ) % 128, 1), last)
        edges[0, tile] = first
        edges[1, tile] = last
    halos = []
    for side in range(2):
        edge_plane = cells_ref.at[rows_of(side * (cells_x - 1)), :]
        halos.append(halo(0, side, edge_plane, planes_in.at[1 - side], (sides_x[side], my)))
        halos.append(halo(0, 2 + side, edges.at[side], edges_in.at[1 - side], (mx, sides_y[side])))
        for other in range(2):
            halos.append(
                halo(
                    0, 4 + 2 * side + other, edges.at[other, side * last_tile],
                    corners_in.at[1 - side, 1 - other], (sides_x[side], sides_y[other]),
                )
            )

    half = lanes // 2
    dot = functools.partial(jnp.dot, preferred_element_type=jnp.float32)
    for copy in fields:
        copy.wait()
    loads[0].wait()
    loads[1].wait()
    sources = [lax.rem(my - step + groups_y, groups_y) for step in range(groups_y)]
    stack = [cells_ref[aligned(my), :]] + [field_in[step] for step in range(1, groups_y)]
    left_high, left_low = split_pair(jnp.concatenate(stack, axis=0))
    copies = [None] * groups_y
    for step in list(range(1, groups_y)) + [0]:
        peer = lax.rem(my + step, groups_y)
        high, low = fwd_high[peer], fwd_low[peer]
        part = dot(left_high, high) + dot(left_high, low) + dot(left_low, high)
        first = jnp.zeros((channels, lanes), jnp.float32)
        second = jnp.zeros((channels, lanes), jnp.float32)
        for place, source in enumerate(sources):
            turn = rotation[source * groups_y + peer]
            piece = part[place * channels : (place + 1) * channels]
            first = first + piece * turn[0:1]
            second = second + piece * turn[1:2]
        slab = first - pltpu.roll(second, half, 1)
        if step:
            parts[step] = slab
            copies[step] = send(1, step, parts.at[step], lines.at[step], (mx, peer))
        else:
            lines[0] = slab
    relays = []
    for step in range(groups_y):
        if step:
            copies[step].wait()
        for hop in range(1, groups_x):
            relay = pltpu.make_async_remote_copy(
                src_ref=lines.at[step], dst_ref=lines_in.at[hop, step],
                send_sem=relay_send.at[hop, step], recv_sem=relay_recv.at[hop, step],
                device_id=(lax.rem(mx + hop, groups_x), my), device_id_type=MESH,
            )
            relay.start()
            relays.append(relay)
    f32 = jnp.float32
    at_x = ((mx > 0).astype(f32), (mx < groups_x - 1).astype(f32))
    at_y = ((my > 0).astype(f32), (my < groups_y - 1).astype(f32))
    for copy in halos:
        copy.wait()

    def fill(plane, main, left, right, left_slot, right_slot, scale):
        padded[plane, :, 0:128] = (
            pltpu.roll(left, (128 - NZ - left_slot * NZ) % 128, 1) * (at_y[0] * scale)
        )
        padded[plane, :, 128 : 128 + plane_lanes] = main * scale
        padded[plane, :, 128 + plane_lanes : 256 + plane_lanes] = (
            pltpu.roll(right, (128 - right_slot * NZ) % 128, 1) * (at_y[1] * scale)
        )

    for x in range(cells_x):
        tile, slot = x // per_tile, x % per_tile
        fill(x + 1, cells_ref[rows_of(x), :], edges_in[0, tile], edges_in[1, tile], slot, slot, 1.0)
    end = per_tile - 1
    fill(0, planes_in[0], corners_in[0, 0], corners_in[0, 1], end, end, at_x[0])
    fill(cells_x + 1, planes_in[1], corners_in[1, 0], corners_in[1, 1], 0, 0, at_x[1])

    def convolve(source, kernel, count, width, start, depth):
        kernel_high, kernel_low = split_pair(kernel)
        total_lanes = source.shape[2]
        depths = lax.broadcasted_iota(jnp.int32, (channels, width), 1) % depth
        for slot in range(count + 4):
            sums[slot, :, 0:width] = jnp.zeros((channels, width), f32)

        def one_plane(plane, carry):
            values = source[plane]
            for tap in range(9):
                shift_y, shift_z = tap // 3 - 1, tap % 3 - 1
                moved = pltpu.roll(values, (-shift_y * depth - shift_z) % total_lanes, 1)
                moved = moved[:, start : start + width]
                if shift_z == -1:
                    moved = jnp.where(depths > 0, moved, 0.0)
                elif shift_z == 1:
                    moved = jnp.where(depths < depth - 1, moved, 0.0)
                high, low = split_pair(moved)
                stack_high[tap * channels : (tap + 1) * channels, 0:width] = high
                stack_low[tap * channels : (tap + 1) * channels, 0:width] = low
            high, low = stack_high[:, 0:width], stack_low[:, 0:width]
            term = dot(kernel_high, high) + dot(kernel_high, low) + dot(kernel_low, high)
            for shift_x in range(3):
                piece = term[shift_x * channels : (shift_x + 1) * channels]
                slot = plane - shift_x + 2
                sums[slot, :, 0:width] = sums[slot, :, 0:width] + piece
            return carry

        lax.fori_loop(0, count + 2, one_plane, 0)

    convolve(padded, stacked(fine_ref), cells_x, plane_lanes, 128, NZ)
    pairs = cells_x // 2
    short = NZ // 2
    for x in range(cells_x):
        fine[x] = jax.nn.gelu(sums[x + 2])
    for pair in range(pairs):
        high, low = split_pair(fine[2 * pair] + fine[2 * pair + 1])
        pooled[pair] = dot(high, pool_ref[...]) + dot(low, pool_ref[...])
    packed = jnp.zeros((channels, 128), f32)
    for pair in range(pairs):
        values = pooled[pair]
        slot = lane_full // short
        packed = jnp.where(slot == pair, pltpu.roll(values, (pair * short - short) % 128, 1), packed)
        packed = jnp.where(slot == pairs + pair, pltpu.roll(values, pair * short, 1), packed)
    rim[...] = packed
    rims = []
    for side in range(2):
        rims.append(
            halo(1, side, pooled.at[side * (pairs - 1)], pooled_in.at[1 - side], (sides_x[side], my))
        )
        rims.append(halo(1, 2 + side, rim, rim_in.at[1 - side], (mx, sides_y[side])))
        for other in range(2):
            rims.append(
                halo(
                    1, 4 + 2 * side + other, rim, rim_corners_in.at[1 - side, 1 - other],
                    (sides_x[side], sides_y[other]),
                )
            )
    for copy in relays:
        copy.wait()
    load_weight.wait()
    lane = lax.broadcasted_iota(jnp.int32, (channels, lanes), 1)
    sign = jnp.where(lane < half, 1.0, -1.0).astype(jnp.float32)
    group = lane // KZ
    row_8 = lax.broadcasted_iota(jnp.int32, (groups, lanes), 0)
    diagonal = lax.rem(row_8 - lax.broadcasted_iota(jnp.int32, (groups, lanes), 1) // KZ + groups, groups)

    def spread(values, index):
        picked = jnp.where(group == index, values, 0.0)
        shift = KZ
        while shift < lanes:
            picked = picked + pltpu.roll(picked, shift, 1)
            shift *= 2
        return picked

    def along_x(terms):
        first = jnp.zeros((channels, lanes), jnp.float32)
        second = jnp.zeros((channels, lanes), jnp.float32)
        for values, position in terms:
            first = first + values * table_x[position]
            second = second + values * table_x[KX * total_x + position]
        return first, pltpu.roll(second, half, 1) * sign

    def shifted(step):
        return lax.rem(mx - step + groups_x, groups_x)

    def mixed_copy(hop, j):
        return pltpu.make_async_remote_copy(
            src_ref=mixed.at[aligned(j), :], dst_ref=mixed_in.at[hop, aligned(j), :],
            send_sem=mixed_send.at[hop, j], recv_sem=mixed_recv.at[hop, j],
            device_id=(lax.rem(mx + hop, groups_x), my), device_id_type=MESH,
        )

    def one_mode(j, carry):
        first, second = along_x(
            (
                lines[step] if hop == 0 else lines_in[hop, step],
                (mx * rows_x + j) * total_x + shifted(hop) * cells_x + sources[step],
            )
            for hop in range(groups_x)
            for step in range(groups_y)
        )
        modes = first + second
        tiles = channels * KZ // lanes
        rows = [jnp.zeros((groups, lanes), jnp.float32) for _ in range(tiles)]
        for k in range(rows_y):
            real, imag = spread(modes, k), spread(modes, rows_y + k)
            for tile in range(tiles):
                columns = pl.ds(tile * lanes, lanes)
                w_real = weight[j, k, 0, :, columns]
                w_imag = weight[j, k, 1, :, columns]
                out_real = jnp.sum(real * w_real - imag * w_imag, axis=0, keepdims=True)
                out_imag = jnp.sum(real * w_imag + imag * w_real, axis=0, keepdims=True)
                rows[tile] = jnp.where(row_8 == k, out_real, rows[tile])
                rows[tile] = jnp.where(row_8 == rows_y + k, out_imag, rows[tile])
        for tile in range(tiles):
            turned = jnp.where(diagonal == 0, rows[tile], 0.0)
            for d in range(1, groups):
                moved = pltpu.roll(pltpu.roll(rows[tile], d, 0), lanes - KZ * d, 1)
                turned = jnp.where(diagonal == d, moved, turned)
            start = pl.multiple_of(j * channels + tile * groups, groups)
            mixed[pl.ds(start, groups), :] = turned
        for hop in range(1, groups_x):
            mixed_copy(hop, j).start()
        return carry

    lax.fori_loop(0, rows_x, one_mode, 0)
    for copy in rims:
        copy.wait()
    inner = short * (pairs + 1)

    def fill_coarse(plane, main, left, right, slot, scale):
        before = pltpu.roll(left, (128 - (pairs + slot) * short) % 128, 1) * at_y[0]
        after = pltpu.roll(right, (inner - slot * short) % 128, 1) * at_y[1]
        values = jnp.where(lane_full < short, before, main)
        values = jnp.where(lane_full // short == pairs + 1, after, values)
        coarse_padded[plane] = values * scale

    for pair in range(pairs):
        fill_coarse(pair + 1, pooled[pair], rim_in[0], rim_in[1], pair, 1.0)
    fill_coarse(0, pooled_in[0], rim_corners_in[0, 0], rim_corners_in[0, 1], pairs - 1, at_x[0])
    fill_coarse(pairs + 1, pooled_in[1], rim_corners_in[1, 0], rim_corners_in[1, 1], 0, at_x[1])
    convolve(coarse_padded, stacked(coarse_ref), pairs, 128, 0, short)
    point_high, point_low = split_pair(point_ref[...])
    for pair in range(pairs):
        high, low = split_pair(jax.nn.gelu(sums[pair + 2, :, 0:128]))
        raised = dot(high, spread_ref[...]) + dot(low, spread_ref[...])
        for x in (2 * pair, 2 * pair + 1):
            joined = jnp.concatenate([fine[x] + raised, cells_ref[rows_of(x), :]], axis=0)
            high, low = split_pair(joined)
            value = dot(point_high, high) + dot(point_high, low) + dot(point_low, high)
            base[rows_of(x), :] = value + bias_ref[...]
    for hop in range(1, groups_x):
        for row in range(rows_x):
            mixed_copy(hop, row).wait()

    def one_line(step, carry):
        place = mx * cells_x + lax.rem(my + step, groups_y)
        first, second = along_x(
            (
                mixed[rows_of(row), :] if hop == 0 else mixed_in[hop, rows_of(row), :],
                (shifted(hop) * rows_x + row) * total_x + place,
            )
            for hop in range(groups_x)
            for row in range(rows_x)
        )
        back[step] = first - second
        return carry

    lax.fori_loop(0, groups_y, one_line, 0)
    copies = [None] + [
        send(3, step, back.at[step], back_in.at[step], (mx, lax.rem(my + step, groups_y)))
        for step in range(1, groups_y)
    ]
    loads[2].wait()
    loads[3].wait()
    result = None
    for step in range(groups_y):
        if step:
            copies[step].wait()
        values = back_in[step] if step else back[0]
        peer = sources[step]
        rolled = pltpu.roll(values, half, 1)
        turned = []
        for tile in range(groups_y):
            turn = rotation[lax.rem(my + tile, groups_y) * groups_y + peer]
            turned.append(values * turn[0:1] - rolled * turn[1:2])
        term = dot_split(jnp.concatenate(turned, axis=0), inv_high[peer], inv_low[peer])
        result = term if result is None else result + term
    for step in range(groups_y):
        ready[step] = result[step * channels : (step + 1) * channels]
    copies = [None] + [
        send(4, step, ready.at[step], ready_in.at[step], (mx, lax.rem(my + step, groups_y)))
        for step in range(1, groups_y)
    ]
    for step in range(groups_y):
        if step:
            copies[step].wait()
        values = ready_in[step] if step else ready[0]
        rows = aligned(sources[step])
        out_ref[rows, :] = jax.nn.gelu(values + base[rows, :])


def stacked(weight):
    rows = [
        jnp.concatenate([weight[9 * plane + tap] for tap in range(9)], axis=1)
        for plane in range(3)
    ]
    return jnp.concatenate(rows, axis=0)


def pooling(cells_y):
    cells = np.arange(cells_y * NZ)
    short = NZ // 2
    place = short + cells // NZ // 2 * short + cells % NZ // 2
    hit = place[:, None] == np.arange(128)[None, :]
    pool = jnp.asarray((hit * 0.125).astype(jnp.bfloat16))
    return pool, jnp.asarray(hit.T.astype(np.float32).astype(jnp.bfloat16))


def layer(
    cells, spectral_weight, conv_fine, conv_coarse, conv_mix, linear_weight, bias_vector, cells_y
):
    cells_x, channels, plane = cells.shape
    rows_x, rows_y = spectral_weight.shape[:2]
    groups_x, groups_y = lax.axis_size("gx"), lax.axis_size("gy")
    lanes = 2 * rows_y * KZ
    tables = spectral_tables(groups_x, groups_y, cells_x, cells_y, rows_y)
    slab_k = (rows_x * channels, lanes)
    f32 = jnp.float32
    vmem = pl.BlockSpec(memory_space=pltpu.VMEM)
    return pl.pallas_call(
        functools.partial(
            spectral_kernel, groups_x, groups_y, cells_x, rows_x, rows_y, channels
        ),
        out_shape=jax.ShapeDtypeStruct((cells_x * channels, plane), f32),
        in_specs=[vmem]
        + [pl.BlockSpec(memory_space=pltpu.HBM)] * 4
        + [vmem]
        + [pl.BlockSpec(memory_space=pltpu.SMEM), pl.BlockSpec(memory_space=pltpu.HBM)]
        + [vmem] * 6,
        out_specs=vmem,
        scratch_shapes=[
            pltpu.VMEM((groups_y, channels, plane), f32),
            pltpu.VMEM((groups_y, channels, lanes), f32),
            pltpu.VMEM((groups_y, channels, lanes), f32),
            pltpu.VMEM((groups_x, groups_y, channels, lanes), f32),
            pltpu.VMEM(slab_k, f32),
            pltpu.VMEM((groups_x, *slab_k), f32),
            pltpu.VMEM((groups_y, channels, lanes), f32),
            pltpu.VMEM((groups_y, channels, lanes), f32),
            pltpu.VMEM((groups_y, channels, plane), f32),
            pltpu.VMEM((groups_y, channels, plane), f32),
            pltpu.VMEM(spectral_weight.shape, f32),
            pltpu.SemaphoreType.DMA((5, max(groups_x, groups_y))),
            pltpu.SemaphoreType.DMA((5, max(groups_x, groups_y))),
            pltpu.SemaphoreType.DMA((groups_x, groups_y)),
            pltpu.SemaphoreType.DMA((groups_x, groups_y)),
            pltpu.SemaphoreType.DMA,
            pltpu.VMEM((2, cells_x * NZ // 128, channels, 128), f32),
            pltpu.VMEM((2, cells_x * NZ // 128, channels, 128), f32),
            pltpu.VMEM((2, channels, plane), f32),
            pltpu.VMEM((2, 2, channels, 128), f32),
            pltpu.VMEM((cells_x + 2, channels, plane + 256), f32),
            pltpu.VMEM((9 * channels, plane), jnp.bfloat16),
            pltpu.VMEM((9 * channels, plane), jnp.bfloat16),
            pltpu.VMEM((cells_x + 4, channels, plane), f32),
            pltpu.VMEM((cells_x, channels, plane), f32),
            pltpu.VMEM((cells_x // 2, channels, 128), f32),
            pltpu.VMEM((channels, 128), f32),
            pltpu.VMEM((2, channels, 128), f32),
            pltpu.VMEM((2, channels, 128), f32),
            pltpu.VMEM((2, 2, channels, 128), f32),
            pltpu.VMEM((cells_x // 2 + 2, channels, 128), f32),
            pltpu.VMEM((cells_x * channels, plane), f32),
            pltpu.SemaphoreType.DMA((2, 8)),
            pltpu.SemaphoreType.DMA((2, 8)),
            *(pltpu.VMEM(table.shape, jnp.bfloat16) for table in tables[:4]),
            pltpu.SemaphoreType.DMA((4,)),
            pltpu.SemaphoreType.DMA((groups_x, rows_x)),
            pltpu.SemaphoreType.DMA((groups_x, rows_x)),
        ],
        compiler_params=pltpu.CompilerParams(
            collective_id=0, has_side_effects=True, vmem_limit_bytes=62 * 1024 * 1024
        ),
    )(
        cells.reshape(cells_x * channels, plane), *tables, spectral_weight,
        conv_fine, conv_coarse,
        jnp.concatenate([conv_mix, linear_weight], axis=1), bias_vector[:, None],
        *pooling(cells_y),
    )


def spectral_general(volume, spectral_weight):
    channels, cells_x, cells_y, _ = volume.shape
    total_x = cells_x * lax.axis_size("gx")
    total_y = cells_y * lax.axis_size("gy")
    merged = channels * KZ
    depth_modes = jnp.arange(KZ, dtype=jnp.int32)
    depth_cells = jnp.arange(NZ, dtype=jnp.int32)
    depth_angles = (depth_cells[:, None] * depth_modes[None, :] % NZ).astype(jnp.float32) * (
        2.0 * math.pi / NZ
    )
    depth_forward = jnp.stack([jnp.cos(depth_angles), -jnp.sin(depth_angles)], axis=1)
    along_z = jnp.einsum("cxyz,zqk->xyqck", volume, depth_forward, precision=exact_precision)
    along_z = along_z.reshape(cells_x, cells_y, 2, merged)
    table_x = forward_table(KX, total_x, lax.axis_index("gx") * cells_x, cells_x)
    table_y = forward_table(KY, total_y, lax.axis_index("gy") * cells_y, cells_y)
    inverse_x = jnp.transpose(table_x, (2, 3, 0, 1))
    inverse_y = jnp.transpose(table_y, (2, 3, 0, 1))
    part_x = jnp.einsum("kpxq,xyqm->kypm", table_x, along_z, precision=exact_precision)
    summed_x = lax.psum_scatter(part_x, "gx", scatter_dimension=0, tiled=True)
    partials = jnp.einsum("jpyq,kyqm->kjpm", table_y, summed_x, precision=exact_precision)
    owned_modes = lax.psum_scatter(partials, "gy", scatter_dimension=1, tiled=True)
    mixed_modes = mix_modes(owned_modes, spectral_weight, channels)
    whole_y = lax.all_gather(mixed_modes, "gy", axis=1, tiled=True)
    back_y = jnp.einsum("ypjq,kjqm->kypm", inverse_y, whole_y, precision=exact_precision)
    whole_x = lax.all_gather(back_y, "gx", axis=0, tiled=True)
    back_x = jnp.einsum("xpkq,kyqm->xypm", inverse_x, whole_x, precision=exact_precision)
    weights_z = jnp.where(depth_modes == 0, 1.0, 2.0).astype(jnp.float32) / (total_x * total_y * NZ)
    inverse_angles = jnp.transpose(depth_angles)
    depth_inverse = jnp.stack(
        [
            weights_z[:, None] * jnp.cos(inverse_angles),
            -weights_z[:, None] * jnp.sin(inverse_angles),
        ],
        axis=0,
    )
    fourier = jnp.einsum(
        "xyqck,qkz->cxyz",
        back_x.reshape(cells_x, cells_y, 2, channels, KZ),
        depth_inverse,
        precision=exact_precision,
    )
    return fourier.reshape(channels, cells_x, cells_y * NZ)


def per_device(
    state_field, spectral_weight, conv_fine, conv_coarse, conv_mix, linear_weight, bias_vector
):
    channels, cells_x, plane = state_field.shape
    cells_y = plane // NZ
    rows_y = spectral_weight.shape[1]
    if (
        2 * rows_y * KZ == 128
        and 2 * rows_y == 8
        and channels * KZ % 128 == 0
        and plane % 128 == 0
        and cells_x % (128 // NZ) == 0
        and cells_x * NZ // 2 == 128
        and cells_x == cells_y == lax.axis_size("gy")
        and min(lax.axis_size("gx"), lax.axis_size("gy")) > 1
    ):
        out = layer(
            jnp.transpose(state_field, (1, 0, 2)), spectral_weight, conv_fine, conv_coarse,
            conv_mix, linear_weight, bias_vector, cells_y,
        )
        return jnp.transpose(out.reshape(cells_x, channels, plane), (1, 0, 2))
    volume = state_field.reshape(channels, cells_x, cells_y, NZ)
    padded = extended(volume, (("gx", 1), ("gy", 2)), 1)
    fine_level = jax.nn.gelu(conv_merged(padded, conv_fine, cells_x, cells_y, NZ))
    pooled = fine_level.reshape(channels, cells_x // 2, 2, cells_y // 2, 2, NZ // 2, 2).mean(
        axis=(2, 4, 6)
    )
    coarse_padded = extended(pooled, (("gx", 1), ("gy", 2)), 1)
    coarse = jax.nn.gelu(
        conv_merged(coarse_padded, conv_coarse, cells_x // 2, cells_y // 2, NZ // 2)
    )
    coarse = coarse.reshape(channels, cells_x // 2, 1, cells_y // 2, 1, NZ // 2, 1)
    spread = jnp.broadcast_to(coarse, (channels, cells_x // 2, 2, cells_y // 2, 2, NZ // 2, 2))
    joined = fine_level + spread.reshape(channels, cells_x, cells_y * NZ)
    unet_branch = jnp.einsum("oi,ixw->oxw", conv_mix, joined, precision=exact_precision)
    pointwise = jnp.einsum("oi,ixw->oxw", linear_weight, state_field, precision=exact_precision)
    fourier = spectral_general(volume, spectral_weight)
    summed = fourier + unet_branch + pointwise + bias_vector[:, None, None]
    return jax.nn.gelu(summed)


def solution(mesh):
    placed = (P(None, "gx", "gy"), P("gx", "gy", None, None, None), P(), P(), P(), P(), P())
    return jax.shard_map(
        per_device, mesh=mesh, in_specs=placed, out_specs=P(None, "gx", "gy"), check_vma=False
    )
```

```python
import functools
import math

import jax
import jax.numpy as jnp
import numpy as np
from jax import lax
from jax.experimental import pallas as pl
from jax.experimental.pallas import tpu as pltpu
from jax.sharding import PartitionSpec as P

KX = 32
KY = 32
KZ = 16
NZ = 32


exact_precision = lax.Precision.HIGH


def extended(cells, sides, width):
    for axis, dim in sides:
        count = lax.axis_size(axis)
        ends = count - 1
        head = lax.slice_in_dim(cells, 0, width, axis=dim)
        tail = lax.slice_in_dim(cells, cells.shape[dim] - width, cells.shape[dim], axis=dim)
        cells = jnp.concatenate(
            [
                lax.ppermute(tail, axis, [(i, (i + 1) % count) for i in range(ends)]),
                cells,
                lax.ppermute(head, axis, [((i + 1) % count, i) for i in range(ends)]),
            ],
            axis=dim,
        )
    return cells


def mode_frequency(count, length):
    indices = jnp.arange(count, dtype=jnp.int32)
    return jnp.where(indices < count // 2, indices, indices - count + length)


def forward_table(count, length, start, cells):
    frequency = mode_frequency(count, length)
    places = start + jnp.arange(cells, dtype=jnp.int32)
    phase = frequency[:, None] * places[None, :] % length
    angles = phase.astype(jnp.float32) * (2.0 * math.pi / length)
    cosines = jnp.cos(angles)
    sines = jnp.sin(angles)
    upper_rows = jnp.stack([cosines, sines], axis=-1)
    lower_rows = jnp.stack([-sines, cosines], axis=-1)
    return jnp.stack([upper_rows, lower_rows], axis=1)


def conv_merged(padded, weight, cells_x, cells_y, depth):
    channels = padded.shape[0]
    flat = padded.reshape(channels, cells_x + 2, (cells_y + 2) * depth)
    flat = jnp.pad(flat, ((0, 0), (0, 0), (1, 1)))
    width = cells_y * depth
    positions = jnp.arange(width, dtype=jnp.int32) % depth
    lower_keep = (positions > 0).astype(jnp.float32)
    upper_keep = (positions < depth - 1).astype(jnp.float32)
    accumulated = jnp.zeros((channels, cells_x, width), jnp.float32)
    for offset in range(27):
        shift_x, shift_y, shift_z = (offset // 9, offset // 3 % 3, offset % 3)
        start = shift_y * depth + shift_z
        window = flat[:, shift_x : shift_x + cells_x, start : start + width]
        term = jnp.einsum("oi,ixw->oxw", weight[offset], window, precision=exact_precision)
        if shift_z == 0:
            term = term * lower_keep
        elif shift_z == 2:
            term = term * upper_keep
        accumulated = accumulated + term
    return accumulated


def contract(values, kernel):
    return jnp.einsum("xyiz,xyioz->xyoz", values, kernel, precision=exact_precision)


def mix_modes(owned_modes, spectral_weight, channels):
    rows_x, rows_y = (owned_modes.shape[0], owned_modes.shape[1])
    values = owned_modes.reshape(rows_x, rows_y, 2, channels, KZ)
    kernel = spectral_weight.reshape(rows_x, rows_y, 2, channels, channels, KZ)
    real_part = contract(values[:, :, 0], kernel[:, :, 0]) - contract(
        values[:, :, 1], kernel[:, :, 1]
    )
    imag_part = contract(values[:, :, 0], kernel[:, :, 1]) + contract(
        values[:, :, 1], kernel[:, :, 0]
    )
    return jnp.stack([real_part, imag_part], axis=2).reshape(rows_x, rows_y, 2, channels * KZ)


MESH = pl.DeviceIdType.MESH


def split_pair(values):
    high = values.astype(jnp.bfloat16)
    return high, (values - high.astype(jnp.float32)).astype(jnp.bfloat16)


def dot_split(left, high, low):
    left_high, left_low = split_pair(left)
    dot = functools.partial(jnp.dot, preferred_element_type=jnp.float32)
    return dot(left_high, high) + dot(left_high, low) + dot(left_low, high)


def host_pair(values):
    high = values.astype(np.float32).astype(jnp.bfloat16)
    low = (values - high.astype(np.float64)).astype(np.float32).astype(jnp.bfloat16)
    return jnp.asarray(high), jnp.asarray(low)


def host_frequency(count, length):
    indices = np.arange(count)
    return np.where(indices < count // 2, indices, indices - count + length)


def spectral_tables(groups_x, groups_y, cells_x, cells_y, rows_y):
    total_x, total_y = groups_x * cells_x, groups_y * cells_y
    fy = host_frequency(KY, total_y)
    places = np.arange(cells_y)
    kz = np.arange(KZ)
    zs = np.arange(NZ)
    turn_y = places[:, None] * fy[None, :] % total_y / total_y
    turn_z = zs[:, None] * kz[None, :] % NZ / NZ
    angle = 2 * np.pi * (turn_y[:, None, :, None] + turn_z[None, :, None, :])
    table = np.stack([np.cos(angle), -np.sin(angle)], axis=2)
    table = table.reshape(cells_y * NZ, 2, groups_y, rows_y, KZ).transpose(2, 0, 1, 3, 4)
    table = table.reshape(groups_y, cells_y * NZ, 2 * rows_y * KZ)
    scale = np.tile(np.where(kz == 0, 1.0, 2.0) / (total_x * total_y * NZ), 2 * rows_y)
    inverse = (table * scale).transpose(0, 2, 1)
    starts = np.arange(groups_y) * cells_y
    phase = 2 * np.pi * (starts[:, None] * fy[None, :] % total_y) / total_y
    phase = np.broadcast_to(phase.reshape(-1, 1, rows_y, 1), (groups_y**2, 2, rows_y, KZ))
    signs = np.array([1.0, -1.0]).reshape(1, 2, 1, 1)
    rotation = np.stack([np.cos(phase), signs * np.sin(phase)], axis=1)
    rotation = rotation.reshape(groups_y**2, 2, 2 * rows_y * KZ).astype(np.float32)
    fx = host_frequency(KX, total_x)
    angle_x = 2 * np.pi * (fx[:, None] * np.arange(total_x)[None, :] % total_x) / total_x
    table_x = np.stack([np.cos(angle_x), np.sin(angle_x)]).reshape(-1).astype(np.float32)
    return (*host_pair(table), *host_pair(inverse), jnp.asarray(rotation), jnp.asarray(table_x))


def lane_group(shape, axis, width):
    return lax.broadcasted_iota(jnp.int32, shape, axis) // width


def spectral_kernel(
    groups_x, groups_y, cells_x, rows_x, rows_y, channels,
    state_ref, fwd_high_hbm, fwd_low_hbm, inv_high_hbm, inv_low_hbm, rotation, table_x, weight_hbm,
    fine_ref, coarse_ref, mix_ref, linear_ref, bias_ref, pool_ref, spread_ref,
    out_ref,
    field_in, parts, lines, lines_in, mixed, mixed_in, back, back_in, ready, ready_in, weight,
    send_sem, recv_sem, relay_send, relay_recv, weight_sem,
    edges, edges_in, planes_in, corners_in, padded, stack_high, stack_low, sums, fine,
    pooled, rim, rim_in, pooled_in, rim_corners_in, coarse_padded, base,
    halo_send, halo_recv, fwd_high, fwd_low, inv_high, inv_low, table_sem,
    mixed_send, mixed_recv, cells_ref,
):
    mx, my = lax.axis_index("gx"), lax.axis_index("gy")
    lanes = 2 * rows_y * KZ
    groups = 2 * rows_y
    total_x = groups_x * cells_x
    load_weight = pltpu.make_async_copy(weight_hbm, weight, weight_sem)
    loads = [
        pltpu.make_async_copy(source, target, table_sem.at[index])
        for index, (source, target) in enumerate(
            (
                (fwd_high_hbm, fwd_high), (fwd_low_hbm, fwd_low),
                (inv_high_hbm, inv_high), (inv_low_hbm, inv_low),
            )
        )
    ]
    for load in loads:
        load.start()
    load_weight.start()
    for x in range(cells_x):
        cells_ref[x * channels : (x + 1) * channels, :] = state_ref[:, x, :]
    barrier = pltpu.get_barrier_semaphore()
    for step in range(1, groups_y):
        pl.semaphore_signal(
            barrier, inc=1, device_id=(mx, lax.rem(my + step, groups_y)), device_id_type=MESH
        )
    for step in range(1, groups_x):
        pl.semaphore_signal(
            barrier, inc=1, device_id=(lax.rem(mx + step, groups_x), my), device_id_type=MESH
        )
    up_x, down_x = lax.rem(mx + 1, groups_x), lax.rem(mx + groups_x - 1, groups_x)
    up_y, down_y = lax.rem(my + 1, groups_y), lax.rem(my + groups_y - 1, groups_y)
    sides_x, sides_y = (down_x, up_x), (down_y, up_y)
    for to_x in sides_x:
        for to_y in sides_y:
            pl.semaphore_signal(barrier, inc=1, device_id=(to_x, to_y), device_id_type=MESH)
    pl.semaphore_wait(barrier, groups_x + groups_y + 2)

    def halo(phase, index, source, target, device):
        copy = pltpu.make_async_remote_copy(
            src_ref=source, dst_ref=target,
            send_sem=halo_send.at[phase, index], recv_sem=halo_recv.at[phase, index],
            device_id=device, device_id_type=MESH,
        )
        copy.start()
        return copy

    def rows_of(plane):
        return pl.ds(plane * channels, channels)

    def send(phase, step, source, target, device):
        copy = pltpu.make_async_remote_copy(
            src_ref=source, dst_ref=target,
            send_sem=send_sem.at[phase, step], recv_sem=recv_sem.at[phase, step],
            device_id=device, device_id_type=MESH,
        )
        copy.start()
        return copy

    def aligned(row):
        return pl.ds(pl.multiple_of(row * channels, channels), channels)

    fields = []
    for step in range(1, groups_y):
        peer = lax.rem(my + step, groups_y)
        fields.append(
            send(0, step, cells_ref.at[aligned(peer), :], field_in.at[step], (mx, peer))
        )
    lane_full = lax.broadcasted_iota(jnp.int32, (channels, 128), 1)
    plane_lanes = cells_ref.shape[1]
    per_tile = 128 // NZ
    last_tile = cells_x // per_tile - 1
    for tile in range(cells_x // per_tile):
        first = jnp.zeros((channels, 128), jnp.float32)
        last = jnp.zeros((channels, 128), jnp.float32)
        for slot in range(per_tile):
            rows = rows_of(tile * per_tile + slot)
            here = lane_full // NZ == slot
            head = cells_ref[rows, 0:128]
            tail = cells_ref[rows, plane_lanes - 128 : plane_lanes]
            first = jnp.where(here, pltpu.roll(head, slot * NZ, 1), first)
            last = jnp.where(here, pltpu.roll(tail, (slot * NZ + NZ) % 128, 1), last)
        edges[0, tile] = first
        edges[1, tile] = last
    halos = []
    for side in range(2):
        edge_plane = cells_ref.at[rows_of(side * (cells_x - 1)), :]
        halos.append(halo(0, side, edge_plane, planes_in.at[1 - side], (sides_x[side], my)))
        halos.append(halo(0, 2 + side, edges.at[side], edges_in.at[1 - side], (mx, sides_y[side])))
        for other in range(2):
            halos.append(
                halo(
                    0, 4 + 2 * side + other, edges.at[other, side * last_tile],
                    corners_in.at[1 - side, 1 - other], (sides_x[side], sides_y[other]),
                )
            )

    half = lanes // 2
    dot = functools.partial(jnp.dot, preferred_element_type=jnp.float32)
    for copy in fields:
        copy.wait()
    loads[0].wait()
    loads[1].wait()
    sources = [lax.rem(my - step + groups_y, groups_y) for step in range(groups_y)]
    stack = [cells_ref[aligned(my), :]] + [field_in[step] for step in range(1, groups_y)]
    left_high, left_low = split_pair(jnp.concatenate(stack, axis=0))
    copies = [None] * groups_y
    for step in list(range(1, groups_y)) + [0]:
        peer = lax.rem(my + step, groups_y)
        high, low = fwd_high[peer], fwd_low[peer]
        part = dot(left_high, high) + dot(left_high, low) + dot(left_low, high)
        first = jnp.zeros((channels, lanes), jnp.float32)
        second = jnp.zeros((channels, lanes), jnp.float32)
        for place, source in enumerate(sources):
            turn = rotation[source * groups_y + peer]
            piece = part[place * channels : (place + 1) * channels]
            first = first + piece * turn[0:1]
            second = second + piece * turn[1:2]
        slab = first - pltpu.roll(second, half, 1)
        if step:
            parts[step] = slab
            copies[step] = send(1, step, parts.at[step], lines.at[step], (mx, peer))
        else:
            lines[0] = slab
    relays = []
    for step in range(groups_y):
        if step:
            copies[step].wait()
        for hop in range(1, groups_x):
            relay = pltpu.make_async_remote_copy(
                src_ref=lines.at[step], dst_ref=lines_in.at[hop, step],
                send_sem=relay_send.at[hop, step], recv_sem=relay_recv.at[hop, step],
                device_id=(lax.rem(mx + hop, groups_x), my), device_id_type=MESH,
            )
            relay.start()
            relays.append(relay)
    f32 = jnp.float32
    at_x = ((mx > 0).astype(f32), (mx < groups_x - 1).astype(f32))
    at_y = ((my > 0).astype(f32), (my < groups_y - 1).astype(f32))
    for copy in halos:
        copy.wait()

    def fill(plane, main, left, right, left_slot, right_slot, scale):
        padded[plane, :, 0:128] = (
            pltpu.roll(left, (128 - NZ - left_slot * NZ) % 128, 1) * (at_y[0] * scale)
        )
        padded[plane, :, 128 : 128 + plane_lanes] = main * scale
        padded[plane, :, 128 + plane_lanes : 256 + plane_lanes] = (
            pltpu.roll(right, (128 - right_slot * NZ) % 128, 1) * (at_y[1] * scale)
        )

    for x in range(cells_x):
        tile, slot = x // per_tile, x % per_tile
        fill(x + 1, cells_ref[rows_of(x), :], edges_in[0, tile], edges_in[1, tile], slot, slot, 1.0)
    end = per_tile - 1
    fill(0, planes_in[0], corners_in[0, 0], corners_in[0, 1], end, end, at_x[0])
    fill(cells_x + 1, planes_in[1], corners_in[1, 0], corners_in[1, 1], 0, 0, at_x[1])

    def convolve(source, kernel, count, width, start, depth):
        kernel_high, kernel_low = split_pair(kernel)
        total_lanes = source.shape[2]
        depths = lax.broadcasted_iota(jnp.int32, (channels, width), 1) % depth
        for slot in range(count + 4):
            sums[slot, :, 0:width] = jnp.zeros((channels, width), f32)

        def one_plane(plane, carry):
            values = source[plane]
            for tap in range(9):
                shift_y, shift_z = tap // 3 - 1, tap % 3 - 1
                moved = pltpu.roll(values, (-shift_y * depth - shift_z) % total_lanes, 1)
                moved = moved[:, start : start + width]
                if shift_z == -1:
                    moved = jnp.where(depths > 0, moved, 0.0)
                elif shift_z == 1:
                    moved = jnp.where(depths < depth - 1, moved, 0.0)
                high, low = split_pair(moved)
                stack_high[tap * channels : (tap + 1) * channels, 0:width] = high
                stack_low[tap * channels : (tap + 1) * channels, 0:width] = low
            high, low = stack_high[:, 0:width], stack_low[:, 0:width]
            term = dot(kernel_high, high) + dot(kernel_high, low) + dot(kernel_low, high)
            for shift_x in range(3):
                piece = term[shift_x * channels : (shift_x + 1) * channels]
                slot = plane - shift_x + 2
                sums[slot, :, 0:width] = sums[slot, :, 0:width] + piece
            return carry

        lax.fori_loop(0, count + 2, one_plane, 0)

    convolve(padded, stacked(fine_ref), cells_x, plane_lanes, 128, NZ)
    pairs = cells_x // 2
    short = NZ // 2
    for x in range(cells_x):
        fine[x] = jax.nn.gelu(sums[x + 2])
    for pair in range(pairs):
        high, low = split_pair(fine[2 * pair] + fine[2 * pair + 1])
        pooled[pair] = dot(high, pool_ref[...]) + dot(low, pool_ref[...])
    packed = jnp.zeros((channels, 128), f32)
    for pair in range(pairs):
        values = pooled[pair]
        slot = lane_full // short
        packed = jnp.where(slot == pair, pltpu.roll(values, (pair * short - short) % 128, 1), packed)
        packed = jnp.where(slot == pairs + pair, pltpu.roll(values, pair * short, 1), packed)
    rim[...] = packed
    rims = []
    for side in range(2):
        rims.append(
            halo(1, side, pooled.at[side * (pairs - 1)], pooled_in.at[1 - side], (sides_x[side], my))
        )
        rims.append(halo(1, 2 + side, rim, rim_in.at[1 - side], (mx, sides_y[side])))
        for other in range(2):
            rims.append(
                halo(
                    1, 4 + 2 * side + other, rim, rim_corners_in.at[1 - side, 1 - other],
                    (sides_x[side], sides_y[other]),
                )
            )
    for copy in relays:
        copy.wait()
    load_weight.wait()
    lane = lax.broadcasted_iota(jnp.int32, (channels, lanes), 1)
    sign = jnp.where(lane < half, 1.0, -1.0).astype(jnp.float32)
    group = lane // KZ
    row_8 = lax.broadcasted_iota(jnp.int32, (groups, lanes), 0)
    diagonal = lax.rem(row_8 - lax.broadcasted_iota(jnp.int32, (groups, lanes), 1) // KZ + groups, groups)

    def spread(values, index):
        picked = jnp.where(group == index, values, 0.0)
        shift = KZ
        while shift < lanes:
            picked = picked + pltpu.roll(picked, shift, 1)
            shift *= 2
        return picked

    def along_x(terms):
        first = jnp.zeros((channels, lanes), jnp.float32)
        second = jnp.zeros((channels, lanes), jnp.float32)
        for values, position in terms:
            first = first + values * table_x[position]
            second = second + values * table_x[KX * total_x + position]
        return first, pltpu.roll(second, half, 1) * sign

    def shifted(step):
        return lax.rem(mx - step + groups_x, groups_x)

    def mixed_copy(hop, j):
        return pltpu.make_async_remote_copy(
            src_ref=mixed.at[aligned(j), :], dst_ref=mixed_in.at[hop, aligned(j), :],
            send_sem=mixed_send.at[hop, j], recv_sem=mixed_recv.at[hop, j],
            device_id=(lax.rem(mx + hop, groups_x), my), device_id_type=MESH,
        )

    def one_mode(j, carry):
        first, second = along_x(
            (
                lines[step] if hop == 0 else lines_in[hop, step],
                (mx * rows_x + j) * total_x + shifted(hop) * cells_x + sources[step],
            )
            for hop in range(groups_x)
            for step in range(groups_y)
        )
        modes = first + second
        tiles = channels * KZ // lanes
        rows = [jnp.zeros((groups, lanes), jnp.float32) for _ in range(tiles)]
        for k in range(rows_y):
            real, imag = spread(modes, k), spread(modes, rows_y + k)
            for tile in range(tiles):
                columns = pl.ds(tile * lanes, lanes)
                w_real = weight[j, k, 0, :, columns]
                w_imag = weight[j, k, 1, :, columns]
                out_real = jnp.sum(real * w_real - imag * w_imag, axis=0, keepdims=True)
                out_imag = jnp.sum(real * w_imag + imag * w_real, axis=0, keepdims=True)
                rows[tile] = jnp.where(row_8 == k, out_real, rows[tile])
                rows[tile] = jnp.where(row_8 == rows_y + k, out_imag, rows[tile])
        for tile in range(tiles):
            turned = jnp.where(diagonal == 0, rows[tile], 0.0)
            for d in range(1, groups):
                moved = pltpu.roll(pltpu.roll(rows[tile], d, 0), lanes - KZ * d, 1)
                turned = jnp.where(diagonal == d, moved, turned)
            start = pl.multiple_of(j * channels + tile * groups, groups)
            mixed[pl.ds(start, groups), :] = turned
        for hop in range(1, groups_x):
            mixed_copy(hop, j).start()
        return carry

    lax.fori_loop(0, rows_x, one_mode, 0)
    for copy in rims:
        copy.wait()
    inner = short * (pairs + 1)

    def fill_coarse(plane, main, left, right, slot, scale):
        before = pltpu.roll(left, (128 - (pairs + slot) * short) % 128, 1) * at_y[0]
        after = pltpu.roll(right, (inner - slot * short) % 128, 1) * at_y[1]
        values = jnp.where(lane_full < short, before, main)
        values = jnp.where(lane_full // short == pairs + 1, after, values)
        coarse_padded[plane] = values * scale

    for pair in range(pairs):
        fill_coarse(pair + 1, pooled[pair], rim_in[0], rim_in[1], pair, 1.0)
    fill_coarse(0, pooled_in[0], rim_corners_in[0, 0], rim_corners_in[0, 1], pairs - 1, at_x[0])
    fill_coarse(pairs + 1, pooled_in[1], rim_corners_in[1, 0], rim_corners_in[1, 1], 0, at_x[1])
    convolve(coarse_padded, stacked(coarse_ref), pairs, 128, 0, short)
    point_high, point_low = split_pair(jnp.concatenate([mix_ref[...], linear_ref[...]], axis=1))
    across = lax.broadcasted_iota(jnp.int32, (channels, channels), 0)
    along = lax.broadcasted_iota(jnp.int32, (channels, channels), 1)
    bias = jnp.sum(jnp.where(across == along, bias_ref[...], 0.0), axis=1, keepdims=True)
    for pair in range(pairs):
        high, low = split_pair(jax.nn.gelu(sums[pair + 2, :, 0:128]))
        raised = dot(high, spread_ref[...]) + dot(low, spread_ref[...])
        for x in (2 * pair, 2 * pair + 1):
            joined = jnp.concatenate([fine[x] + raised, cells_ref[rows_of(x), :]], axis=0)
            high, low = split_pair(joined)
            value = dot(point_high, high) + dot(point_high, low) + dot(point_low, high)
            base[rows_of(x), :] = value + bias
    for hop in range(1, groups_x):
        for row in range(rows_x):
            mixed_copy(hop, row).wait()

    def one_line(step, carry):
        place = mx * cells_x + lax.rem(my + step, groups_y)
        first, second = along_x(
            (
                mixed[rows_of(row), :] if hop == 0 else mixed_in[hop, rows_of(row), :],
                (shifted(hop) * rows_x + row) * total_x + place,
            )
            for hop in range(groups_x)
            for row in range(rows_x)
        )
        back[step] = first - second
        return carry

    lax.fori_loop(0, groups_y, one_line, 0)
    copies = [None] + [
        send(3, step, back.at[step], back_in.at[step], (mx, lax.rem(my + step, groups_y)))
        for step in range(1, groups_y)
    ]
    loads[2].wait()
    loads[3].wait()
    result = None
    for step in range(groups_y):
        if step:
            copies[step].wait()
        values = back_in[step] if step else back[0]
        peer = sources[step]
        rolled = pltpu.roll(values, half, 1)
        turned = []
        for tile in range(groups_y):
            turn = rotation[lax.rem(my + tile, groups_y) * groups_y + peer]
            turned.append(values * turn[0:1] - rolled * turn[1:2])
        term = dot_split(jnp.concatenate(turned, axis=0), inv_high[peer], inv_low[peer])
        result = term if result is None else result + term
    for step in range(groups_y):
        ready[step] = result[step * channels : (step + 1) * channels]
    copies = [None] + [
        send(4, step, ready.at[step], ready_in.at[step], (mx, lax.rem(my + step, groups_y)))
        for step in range(1, groups_y)
    ]
    for step in range(groups_y):
        if step:
            copies[step].wait()
        values = ready_in[step] if step else ready[0]
        rows = aligned(sources[step])
        out_ref[rows, :] = jax.nn.gelu(values + base[rows, :])


def stacked(weight):
    rows = [
        jnp.concatenate([weight[9 * plane + tap] for tap in range(9)], axis=1)
        for plane in range(3)
    ]
    return jnp.concatenate(rows, axis=0)


def pooling(cells_y):
    cells = np.arange(cells_y * NZ)
    short = NZ // 2
    place = short + cells // NZ // 2 * short + cells % NZ // 2
    hit = place[:, None] == np.arange(128)[None, :]
    pool = jnp.asarray((hit * 0.125).astype(jnp.bfloat16))
    return pool, jnp.asarray(hit.T.astype(np.float32).astype(jnp.bfloat16))


def layer(
    cells, spectral_weight, conv_fine, conv_coarse, conv_mix, linear_weight, bias_vector, cells_y
):
    channels, cells_x, plane = cells.shape
    rows_x, rows_y = spectral_weight.shape[:2]
    groups_x, groups_y = lax.axis_size("gx"), lax.axis_size("gy")
    lanes = 2 * rows_y * KZ
    tables = spectral_tables(groups_x, groups_y, cells_x, cells_y, rows_y)
    slab_k = (rows_x * channels, lanes)
    f32 = jnp.float32
    vmem = pl.BlockSpec(memory_space=pltpu.VMEM)
    return pl.pallas_call(
        functools.partial(
            spectral_kernel, groups_x, groups_y, cells_x, rows_x, rows_y, channels
        ),
        out_shape=jax.ShapeDtypeStruct((cells_x * channels, plane), f32),
        in_specs=[vmem]
        + [pl.BlockSpec(memory_space=pltpu.HBM)] * 4
        + [vmem]
        + [pl.BlockSpec(memory_space=pltpu.SMEM), pl.BlockSpec(memory_space=pltpu.HBM)]
        + [vmem] * 7,
        out_specs=vmem,
        scratch_shapes=[
            pltpu.VMEM((groups_y, channels, plane), f32),
            pltpu.VMEM((groups_y, channels, lanes), f32),
            pltpu.VMEM((groups_y, channels, lanes), f32),
            pltpu.VMEM((groups_x, groups_y, channels, lanes), f32),
            pltpu.VMEM(slab_k, f32),
            pltpu.VMEM((groups_x, *slab_k), f32),
            pltpu.VMEM((groups_y, channels, lanes), f32),
            pltpu.VMEM((groups_y, channels, lanes), f32),
            pltpu.VMEM((groups_y, channels, plane), f32),
            pltpu.VMEM((groups_y, channels, plane), f32),
            pltpu.VMEM(spectral_weight.shape, f32),
            pltpu.SemaphoreType.DMA((5, max(groups_x, groups_y))),
            pltpu.SemaphoreType.DMA((5, max(groups_x, groups_y))),
            pltpu.SemaphoreType.DMA((groups_x, groups_y)),
            pltpu.SemaphoreType.DMA((groups_x, groups_y)),
            pltpu.SemaphoreType.DMA,
            pltpu.VMEM((2, cells_x * NZ // 128, channels, 128), f32),
            pltpu.VMEM((2, cells_x * NZ // 128, channels, 128), f32),
            pltpu.VMEM((2, channels, plane), f32),
            pltpu.VMEM((2, 2, channels, 128), f32),
            pltpu.VMEM((cells_x + 2, channels, plane + 256), f32),
            pltpu.VMEM((9 * channels, plane), jnp.bfloat16),
            pltpu.VMEM((9 * channels, plane), jnp.bfloat16),
            pltpu.VMEM((cells_x + 4, channels, plane), f32),
            pltpu.VMEM((cells_x, channels, plane), f32),
            pltpu.VMEM((cells_x // 2, channels, 128), f32),
            pltpu.VMEM((channels, 128), f32),
            pltpu.VMEM((2, channels, 128), f32),
            pltpu.VMEM((2, channels, 128), f32),
            pltpu.VMEM((2, 2, channels, 128), f32),
            pltpu.VMEM((cells_x // 2 + 2, channels, 128), f32),
            pltpu.VMEM((cells_x * channels, plane), f32),
            pltpu.SemaphoreType.DMA((2, 8)),
            pltpu.SemaphoreType.DMA((2, 8)),
            *(pltpu.VMEM(table.shape, jnp.bfloat16) for table in tables[:4]),
            pltpu.SemaphoreType.DMA((4,)),
            pltpu.SemaphoreType.DMA((groups_x, rows_x)),
            pltpu.SemaphoreType.DMA((groups_x, rows_x)),
            pltpu.VMEM((cells_x * channels, plane), f32),
        ],
        compiler_params=pltpu.CompilerParams(
            collective_id=0, has_side_effects=True, vmem_limit_bytes=62 * 1024 * 1024
        ),
    )(
        cells, *tables, spectral_weight,
        conv_fine, conv_coarse,
        conv_mix, linear_weight, bias_vector.reshape(1, channels),
        *pooling(cells_y),
    )


def spectral_general(volume, spectral_weight):
    channels, cells_x, cells_y, _ = volume.shape
    total_x = cells_x * lax.axis_size("gx")
    total_y = cells_y * lax.axis_size("gy")
    merged = channels * KZ
    depth_modes = jnp.arange(KZ, dtype=jnp.int32)
    depth_cells = jnp.arange(NZ, dtype=jnp.int32)
    depth_angles = (depth_cells[:, None] * depth_modes[None, :] % NZ).astype(jnp.float32) * (
        2.0 * math.pi / NZ
    )
    depth_forward = jnp.stack([jnp.cos(depth_angles), -jnp.sin(depth_angles)], axis=1)
    along_z = jnp.einsum("cxyz,zqk->xyqck", volume, depth_forward, precision=exact_precision)
    along_z = along_z.reshape(cells_x, cells_y, 2, merged)
    table_x = forward_table(KX, total_x, lax.axis_index("gx") * cells_x, cells_x)
    table_y = forward_table(KY, total_y, lax.axis_index("gy") * cells_y, cells_y)
    inverse_x = jnp.transpose(table_x, (2, 3, 0, 1))
    inverse_y = jnp.transpose(table_y, (2, 3, 0, 1))
    part_x = jnp.einsum("kpxq,xyqm->kypm", table_x, along_z, precision=exact_precision)
    summed_x = lax.psum_scatter(part_x, "gx", scatter_dimension=0, tiled=True)
    partials = jnp.einsum("jpyq,kyqm->kjpm", table_y, summed_x, precision=exact_precision)
    owned_modes = lax.psum_scatter(partials, "gy", scatter_dimension=1, tiled=True)
    mixed_modes = mix_modes(owned_modes, spectral_weight, channels)
    whole_y = lax.all_gather(mixed_modes, "gy", axis=1, tiled=True)
    back_y = jnp.einsum("ypjq,kjqm->kypm", inverse_y, whole_y, precision=exact_precision)
    whole_x = lax.all_gather(back_y, "gx", axis=0, tiled=True)
    back_x = jnp.einsum("xpkq,kyqm->xypm", inverse_x, whole_x, precision=exact_precision)
    weights_z = jnp.where(depth_modes == 0, 1.0, 2.0).astype(jnp.float32) / (total_x * total_y * NZ)
    inverse_angles = jnp.transpose(depth_angles)
    depth_inverse = jnp.stack(
        [
            weights_z[:, None] * jnp.cos(inverse_angles),
            -weights_z[:, None] * jnp.sin(inverse_angles),
        ],
        axis=0,
    )
    fourier = jnp.einsum(
        "xyqck,qkz->cxyz",
        back_x.reshape(cells_x, cells_y, 2, channels, KZ),
        depth_inverse,
        precision=exact_precision,
    )
    return fourier.reshape(channels, cells_x, cells_y * NZ)


def per_device(
    state_field, spectral_weight, conv_fine, conv_coarse, conv_mix, linear_weight, bias_vector
):
    channels, cells_x, plane = state_field.shape
    cells_y = plane // NZ
    rows_y = spectral_weight.shape[1]
    if (
        2 * rows_y * KZ == 128
        and 2 * rows_y == 8
        and channels * KZ % 128 == 0
        and plane % 128 == 0
        and cells_x % (128 // NZ) == 0
        and cells_x * NZ // 2 == 128
        and cells_x == cells_y == lax.axis_size("gy")
        and min(lax.axis_size("gx"), lax.axis_size("gy")) > 1
    ):
        out = layer(
            state_field, spectral_weight, conv_fine, conv_coarse,
            conv_mix, linear_weight, bias_vector, cells_y,
        )
        return jnp.transpose(out.reshape(cells_x, channels, plane), (1, 0, 2))
    volume = state_field.reshape(channels, cells_x, cells_y, NZ)
    padded = extended(volume, (("gx", 1), ("gy", 2)), 1)
    fine_level = jax.nn.gelu(conv_merged(padded, conv_fine, cells_x, cells_y, NZ))
    pooled = fine_level.reshape(channels, cells_x // 2, 2, cells_y // 2, 2, NZ // 2, 2).mean(
        axis=(2, 4, 6)
    )
    coarse_padded = extended(pooled, (("gx", 1), ("gy", 2)), 1)
    coarse = jax.nn.gelu(
        conv_merged(coarse_padded, conv_coarse, cells_x // 2, cells_y // 2, NZ // 2)
    )
    coarse = coarse.reshape(channels, cells_x // 2, 1, cells_y // 2, 1, NZ // 2, 1)
    spread = jnp.broadcast_to(coarse, (channels, cells_x // 2, 2, cells_y // 2, 2, NZ // 2, 2))
    joined = fine_level + spread.reshape(channels, cells_x, cells_y * NZ)
    unet_branch = jnp.einsum("oi,ixw->oxw", conv_mix, joined, precision=exact_precision)
    pointwise = jnp.einsum("oi,ixw->oxw", linear_weight, state_field, precision=exact_precision)
    fourier = spectral_general(volume, spectral_weight)
    summed = fourier + unet_branch + pointwise + bias_vector[:, None, None]
    return jax.nn.gelu(summed)


def solution(mesh):
    placed = (P(None, "gx", "gy"), P("gx", "gy", None, None, None), P(), P(), P(), P(), P())
    return jax.shard_map(
        per_device, mesh=mesh, in_specs=placed, out_specs=P(None, "gx", "gy"), check_vma=False
    )
```
